128 devices in a mesh: seq: 32 (over y_hi, x, z), batch: 4 (over y_lo, core).
Axes of the slice: x: 4, y: 4 (y_hi: 2, y_lo: 2; y = y_hi * 2 + y_lo), z: 4, core: 2. Of those that a mesh axis runs over, the one named last changes fastest.
Arguments:
- tokens: bfloat16 [4, 8192, 256], P('batch', 'seq'), may hold values from -6 to 6
- out_grad: bfloat16 [4, 8192, 256], P('batch', 'seq'), may hold values from -6 to 6
- in_weight: bfloat16 [256, 768], replicated, may hold values from -0.375 to 0.375
- out_weight: bfloat16 [256, 256], replicated, may hold values from -0.375 to 0.375
- skip_bias: float32 [256], replicated, may hold values from -4 to 4
- embed_weight: float32 [5, 64], replicated, may hold values from -4 to 4
- embed_bias: float32 [64], replicated, may hold values from -4 to 4
- hidden_weight: float32 [64, 64], replicated, may hold values from -0.75 to 0.75
- hidden_bias: float32 [64], replicated, may hold values from -4 to 4
- filter_weight: float32 [64, 256], replicated, may hold values from -0.75 to 0.75
- sine_freq: float32 [2, 64], replicated, may hold values from 0.5 to 3
- decay_rate: float32 [256], replicated, may hold values from 0.00037475585 to 0.0018737793
Outputs:
- grad_tokens: bfloat16 [4, 8192, 256], P('batch', 'seq')
- grad_in_weight: float32 [256, 768], replicated
- grad_out_weight: float32 [256, 256], replicated
- grad_skip_bias: float32 [256], replicated
- grad_embed_weight: float32 [5, 64], replicated
- grad_embed_bias: float32 [64], replicated
- grad_hidden_weight: float32 [64, 64], replicated
- grad_hidden_bias: float32 [64], replicated
- grad_filter_weight: float32 [64, 256], replicated
- grad_sine_freq: float32 [2, 64], replicated
The draws below stay inside these ranges and needn't reach their ends.
All inputs are finite; a program needn't handle non-finite values.
Results may differ from the reference program's by a relative error of at most 0.013.
Values may be sent and summed in bfloat16 or wider, within the bound.
No kernel may reach another device: no remote copies, remote signals or barrier semaphores. Data moves between devices by JAX's collectives and lax.ppermute only.
A program may use at most 64 MiB of HBM per device.

```python
import math
import jax
import jax.numpy as jnp
from jax import lax

D = 256
HID = 64
EMB = 5
BATCH = 4
LEN = 8192


def block_scale(own_key, dims, pieces, least, high):
    def one(dim, parts):
        heights = jax.random.uniform(jax.random.fold_in(jax.random.fold_in(own_key, 6), dim), (parts,), jnp.float32, least / len(pieces), high / len(pieces))
        return jnp.repeat(jnp.exp(heights), dims[dim] // parts).reshape((-1,) + (1,) * (len(dims) - dim - 1))

    gain = one(*pieces[0])
    for cut in pieces[1:]:
        gain = gain * one(*cut)
    return gain


def gaussian(key, dims, spread, reach, shards=(), kind=jnp.bfloat16):
    entries = jax.random.normal(key, dims, jnp.float32) * spread
    if len(shards) > 0:
        entries = block_scale(key, dims, shards, -0.22, 0.18) * entries
    return jnp.clip(entries, min=-reach, max=reach).astype(kind)


def setup_inputs(seed: int = 0) -> dict:
    splits = jax.random.split(jax.random.key(seed), 13)
    return {
        "tokens": gaussian(splits[0], (BATCH, LEN, D), 1.0, 6.0, ((0, 4), (1, 32))),
        "out_grad": gaussian(splits[1], (BATCH, LEN, D), 1.0, 6.0, ((0, 4), (1, 32))),
        "in_weight": gaussian(splits[2], (D, 3 * D), D ** -0.5, 0.375),
        "out_weight": gaussian(splits[3], (D, D), D ** -0.5, 0.375),
        "skip_bias": gaussian(splits[4], (D,), 1.0, 4.0, (), jnp.float32),
        "embed_weight": gaussian(splits[5], (EMB, HID), 1.0, 4.0, (), jnp.float32),
        "embed_bias": gaussian(splits[6], (HID,), 1.0, 4.0, (), jnp.float32),
        "hidden_weight": gaussian(splits[7], (HID, HID), HID ** -0.5, 0.75, (), jnp.float32),
        "hidden_bias": gaussian(splits[8], (HID,), 1.0, 4.0, (), jnp.float32),
        "filter_weight": gaussian(splits[9], (HID, D), HID ** -0.5, 0.75, (), jnp.float32),
        "sine_freq": jnp.clip(jax.random.uniform(splits[10], (2, HID), jnp.float32, 0.5, 3.0), 0.5, 3.0),
        "decay_rate": jnp.clip(jnp.exp(jax.random.uniform(splits[11], (D,), jnp.float32, math.log(0.00037475585), math.log(0.0018737793))), 0.00037475585, 0.0018737793),
    }


highest = lax.Precision.HIGHEST

def embedding(positions, length, band_count):
    scaled = positions / length
    rows_list = [scaled]
    for band_index in range(1, band_count + 1):
        angle = 2.0 * math.pi * band_index * scaled
        rows_list.append(jnp.cos(angle))
        rows_list.append(jnp.sin(angle))
    return jnp.stack(rows_list, axis=1)

def reference(tokens, out_grad, in_weight, out_weight, skip_bias, embed_weight, embed_bias, hidden_weight, hidden_bias, filter_weight, sine_freq, decay_rate):
    positions = jnp.arange(LEN, dtype=jnp.float32)
    band_count = (EMB - 1) // 2
    embed_rows = embedding(positions, LEN, band_count)
    modul = 4.0 * jnp.exp(-decay_rate[None, :] * positions[:, None]) / math.sqrt(LEN)

    def filter_net(weight_one, bias_one, weight_two, bias_two, weight_three, freqs):
        pre_one = jnp.dot(embed_rows, weight_one, precision=highest) + bias_one
        act_one = jnp.sin(freqs[0] * pre_one)
        pre_two = jnp.dot(act_one, weight_two, precision=highest) + bias_two
        act_two = jnp.sin(freqs[1] * pre_two)
        return jnp.dot(act_two, weight_three, precision=highest) * modul
    filt, pullback = jax.vjp(filter_net, embed_weight, embed_bias, hidden_weight, hidden_bias, filter_weight, sine_freq)
    total = 2 * LEN
    filt_spec = jnp.fft.rfft(filt, n=total, axis=0)

    def one_sequence(inputs):
        tokens_one, grads_one = inputs
        projected = jnp.dot(tokens_one, in_weight, preferred_element_type=jnp.float32)
        gate_out = projected[:, :D].astype(jnp.bfloat16)
        gate_in = projected[:, D:2 * D].astype(jnp.bfloat16)
        values_in = projected[:, 2 * D:].astype(jnp.bfloat16)
        mixed = (values_in.astype(jnp.float32) * gate_in.astype(jnp.float32)).astype(jnp.bfloat16)
        grad_gated = jnp.dot(grads_one, out_weight.T, preferred_element_type=jnp.float32).astype(jnp.bfloat16)
        grad_conv = (grad_gated.astype(jnp.float32) * gate_out.astype(jnp.float32)).astype(jnp.bfloat16)
        mixed_float = mixed.astype(jnp.float32)
        grad_float = grad_conv.astype(jnp.float32)
        mixed_spec = jnp.fft.rfft(mixed_float, n=total, axis=0)
        grad_spec = jnp.fft.rfft(grad_float, n=total, axis=0)
        conv = jnp.fft.irfft(mixed_spec * filt_spec, n=total, axis=0)[:LEN]
        conv = (conv + skip_bias[None, :] * mixed_float).astype(jnp.bfloat16)
        grad_mixed = jnp.fft.irfft(grad_spec * jnp.conj(filt_spec), n=total, axis=0)[:LEN]
        grad_mixed = (grad_mixed + skip_bias[None, :] * grad_float).astype(jnp.bfloat16)
        grad_filt = jnp.fft.irfft(grad_spec * jnp.conj(mixed_spec), n=total, axis=0)[:LEN]
        conv_float = conv.astype(jnp.float32)
        gated = (gate_out.astype(jnp.float32) * conv_float).astype(jnp.bfloat16)
        grad_out_w = jnp.dot(gated.T, grads_one, preferred_element_type=jnp.float32)
        grad_gate_out = (grad_gated.astype(jnp.float32) * conv_float).astype(jnp.bfloat16)
        grad_gate_in = (grad_mixed.astype(jnp.float32) * values_in.astype(jnp.float32)).astype(jnp.bfloat16)
        grad_values = (grad_mixed.astype(jnp.float32) * gate_in.astype(jnp.float32)).astype(jnp.bfloat16)
        grad_proj = jnp.concatenate([grad_gate_out, grad_gate_in, grad_values], axis=1)
        grad_tok = jnp.dot(grad_proj, in_weight.T, preferred_element_type=jnp.float32).astype(jnp.bfloat16)
        grad_in_w = jnp.dot(tokens_one.T, grad_proj, preferred_element_type=jnp.float32)
        grad_bias = lax.optimization_barrier(jnp.sum(grad_float * mixed_float, axis=0))
        return (grad_tok, grad_in_w, grad_out_w, grad_bias, grad_filt)
    results = lax.map(one_sequence, (tokens, out_grad))
    grad_scale = 1.0 / math.sqrt(BATCH * LEN)
    filter_scale = grad_scale / 4.0
    grad_filt_total = lax.optimization_barrier(jnp.sum(results[4], axis=0))
    filter_grads = pullback(grad_filt_total)
    return (results[0], lax.optimization_barrier(jnp.sum(results[1], axis=0)) * grad_scale, lax.optimization_barrier(jnp.sum(results[2], axis=0)) * grad_scale, lax.optimization_barrier(jnp.sum(results[3], axis=0)) * grad_scale, filter_grads[0] * filter_scale, filter_grads[1] * filter_scale, filter_grads[2] * filter_scale, filter_grads[3] * filter_scale, filter_grads[4] * filter_scale, filter_grads[5] * filter_scale)
```

```python
import math

import jax
import jax.numpy as jnp
from jax import lax
from jax.experimental import pallas as pl
from jax.experimental.pallas import tpu as pltpu
from jax.sharding import PartitionSpec as P

F32 = jnp.float32
BF16 = jnp.bfloat16
HIGHEST = lax.Precision.HIGHEST
AXES = ("seq", "batch")
LENGTH = 8192
BANDS = 2
NN = (((1,), (0,)), ((), ()))
NT = (((1,), (1,)), ((), ()))


def mm(a, b, dims=NN):
    return lax.dot_general(a, b, dims, preferred_element_type=F32)


def mm_full(a, b, dims=NN):
    return lax.dot_general(a, b, dims, precision=HIGHEST, preferred_element_type=F32)


def iota(shape, dim):
    return lax.broadcasted_iota(jnp.int32, shape, dim)


def one_hot(cond):
    return jnp.where(cond, 1.0, 0.0).astype(BF16)


def own_index():
    return lax.axis_index("seq") * lax.axis_size("batch") + lax.axis_index("batch")


def modulation(decay, first, shape):
    pos = (first + iota(shape, 0)).astype(F32)
    return 4.0 * jnp.exp(-decay * pos) / math.sqrt(LENGTH)


def forward_kernel(
    tok, og, wi, wo, ew, eb, hw, hb, fw, sf, dr,
    slab, go_o, gi_o, v_o, gg_o, bias_o, emb_o, pre1_o, act1_o, pre2_o, act2_o, scr,
):
    first = own_index() * 64
    proj = mm(tok[...], wi[...])
    go = proj[:, :256].astype(BF16)
    gi = proj[:, 256:512].astype(BF16)
    v = proj[:, 512:].astype(BF16)
    gg = mm(og[...], wo[...], NT).astype(BF16)
    go_o[...] = go
    gi_o[...] = gi
    v_o[...] = v
    gg_o[...] = gg
    mixed = (v.astype(F32) * gi.astype(F32)).astype(BF16).astype(F32)
    gc = (gg.astype(F32) * go.astype(F32)).astype(BF16).astype(F32)
    bias_o[...] = jnp.sum(gc * mixed, axis=0, keepdims=True)
    mixed_t = mixed.T
    gc_t = gc.T
    scaled = (first + iota((64, 64), 0)).astype(F32) / LENGTH
    rows = [scaled]
    for band in range(1, BANDS + 1):
        angle = 2.0 * math.pi * band * scaled
        rows.append(jnp.cos(angle))
        rows.append(jnp.sin(angle))
    pre1 = eb[...]
    for k in range(5):
        pre1 = pre1 + rows[k] * ew[k : k + 1, :]
        emb_o[k] = rows[k]
    act1 = jnp.sin(sf[0:1, :] * pre1)
    pre2 = mm_full(act1, hw[...]) + hb[...]
    act2 = jnp.sin(sf[1:2, :] * pre2)
    pre1_o[...] = pre1
    act1_o[...] = act1
    pre2_o[...] = pre2
    act2_o[...] = act2
    filt = mm_full(act2, fw[...]) * modulation(dr[...], first, (64, 256))
    place = one_hot(iota((64, 256), 1) == iota((64, 256), 0) + 64 * lax.axis_index("batch"))
    filt_t = mm(filt.T.astype(BF16), place)
    for at, whole in ((0, mixed_t), (4, gc_t), (8, filt_t)):
        for ch in range(2):
            for half in range(2):
                scr[:, at + 2 * ch + half, :] = whole[
                    128 * ch : 128 * ch + 128, 128 * half : 128 * half + 128
                ]
    slab[...] = scr[...].astype(BF16)


def conv_kernel(recv, skip, out, scr, osc, spad, spad_odd, fscr, acc, gpad, gs, gsc):
    scr[...] = recv[...].astype(F32)
    own = own_index()
    rev256 = one_hot(iota((256, 256), 0) + iota((256, 256), 1) == 255)
    rev128 = one_hot(iota((128, 128), 0) + iota((128, 128), 1) == 127)

    def order(row, col):
        blk, sig = row // 8, row % 8
        return (row >= 0) & (
            jnp.where(sig < 4, blk * 4 + sig, 128 + (31 - blk) * 4 + sig - 4) == col
        )

    row, col = iota((256, 256), 0), iota((256, 256), 1)
    perm = one_hot(order(row, col))
    perm_odd = one_hot(order(row - 8, col))
    back = one_hot(order(col, row))
    gather_f = one_hot(iota((256, 128), 1) // 4 == iota((256, 128), 0) // 8)
    spread_g = one_hot(iota((128, 64), 0) // 2 == iota((128, 64), 1))
    lane, sub = iota((128, 128), 1), iota((128, 128), 0)
    upper = lane >= sub
    keep = lane <= sub
    spad[0:256, :] = jnp.zeros((256, 256), BF16)
    spad_odd[0:256, :] = jnp.zeros((256, 256), BF16)
    for ch in range(2):
        xs = [scr[:, 2 * ch + h, :] for h in range(2)]
        gs_in = [scr[:, 4 + 2 * ch + h, :] for h in range(2)]
        fs = [scr[:, 8 + 2 * ch + h, :] for h in range(2)]
        x2 = jnp.concatenate(xs, axis=1).astype(BF16)
        g2 = jnp.concatenate(gs_in, axis=1).astype(BF16)
        g_rev = mm(g2, rev256).astype(BF16)
        both = jnp.concatenate([x2, g_rev], axis=0)
        spad[256:512, :] = mm(perm, both).astype(BF16)
        spad_odd[256:512, :] = mm(perm_odd, both).astype(BF16)
        fscr[...] = mm(gather_f, jnp.concatenate(fs, axis=1).astype(BF16))
        acc[...] = jnp.zeros((256, 256), F32)

        def conv_step(m, carry):
            w_last, u_last = carry
            us = [u_last]
            for n in range(4):
                at = pl.multiple_of(16 * m + 8 * (n // 2), 8)
                line = fscr[pl.ds(at, 8), 128 * (n % 2) : 128 * (n % 2) + 128]
                w = pltpu.roll(
                    jnp.concatenate([line] * 16, axis=0), 0, 1, stride=1, stride_axis=0
                )
                us.append(jnp.where(upper, w, w_last).astype(BF16))
                w_last = w
            toep = jnp.concatenate(
                [
                    jnp.concatenate([us[1], us[2]], axis=1),
                    jnp.concatenate([us[0], us[1]], axis=1),
                    jnp.concatenate([us[3], us[4]], axis=1),
                    jnp.concatenate([us[2], us[3]], axis=1),
                ],
                axis=0,
            )
            at = pl.multiple_of(256 - 16 * m, 16)
            left = jnp.concatenate(
                [spad[pl.ds(at, 256), :], spad_odd[pl.ds(at, 256), :]], axis=1
            )
            acc[...] += mm(left, toep)
            return (w_last, us[4])

        lax.fori_loop(
            0, 16, conv_step, (jnp.zeros((128, 128), F32), jnp.zeros((128, 128), BF16))
        )
        skip_now = skip[own + 128 * ch]
        done = (acc[...] + skip_now * spad[256:512, :].astype(F32)).astype(BF16)
        apart = mm(back, done)
        conv2 = apart[0:128, :]
        gm2 = mm(apart[128:256, :].astype(BF16), rev256)
        for h in range(2):
            osc[:, 2 * ch + h, :] = conv2[:, 128 * h : 128 * h + 128]
            osc[:, 4 + 2 * ch + h, :] = gm2[:, 128 * h : 128 * h + 128]

        x_rev = jnp.concatenate(
            [mm(rev128, x.astype(BF16), NT).astype(BF16) for x in xs], axis=1
        )
        for h in range(2):
            gpad[0:128, :] = gs_in[h]
            gpad[128:288, :] = jnp.zeros((160, 128), F32)
            for s in range(4):
                gs[4 * h + s] = gpad[4 * s : 4 * s + 256, :].astype(BF16)

        def corr_step(q, d_last):
            for s in range(4):
                at = pl.multiple_of(16 * q, 16)
                at_next = pl.multiple_of(16 * q + 16 * (s // 3), 16)
                g0 = gs[s, pl.ds(at, 128), :]
                g1 = gs[4 + s, pl.ds(at, 128), :]
                g0_next = gs[(s + 1) % 4, pl.ds(at_next, 128), :]
                right = jnp.concatenate(
                    [
                        jnp.concatenate([g0, g1], axis=1),
                        jnp.concatenate([g1, g0_next], axis=1),
                    ],
                    axis=0,
                )
                c = mm(x_rev, right)
                for odd in range(2):
                    d = pltpu.roll(
                        c[:, 128 * odd : 128 * odd + 128], 1, 1, stride=1, stride_axis=0
                    )
                    part = jnp.where(keep, d_last, d).reshape(16, 8, 128).sum(axis=0)
                    gsc[pl.ds(pl.multiple_of(64 * q + 8 * (2 * s + odd), 8), 8), :] = part
                    d_last = d
            return d_last

        d_end = lax.fori_loop(0, 8, corr_step, jnp.zeros((128, 128), F32))
        gsc[512:520, :] = jnp.where(keep, d_end, 0.0).reshape(16, 8, 128).sum(axis=0)
        gf = gsc[8:520, :].reshape(64, 8, 128).sum(axis=1)
        hi = gf.astype(BF16)
        lo = (gf - hi.astype(F32)).astype(BF16)
        osc[:, 8 + ch, :] = mm(spread_g, hi)
        osc[:, 10 + ch, :] = mm(spread_g, lo)
    out[...] = osc[...].astype(BF16)


def backward_kernel(
    recv, go, gi, v, gg, tok, og, wi, emb, pre1, act1, pre2, act2, bias, hw, fw, sf, dr,
    gtok, slab, scr, tmp, sm, ssc,
):
    own = own_index()
    first = own * 64
    scr[...] = recv[...].astype(F32)

    def whole(at):
        return jnp.concatenate(
            [
                jnp.concatenate([scr[:, at + 2 * ch, :], scr[:, at + 2 * ch + 1, :]], axis=1)
                for ch in range(2)
            ],
            axis=0,
        )

    conv = whole(0).T
    gm = whole(4).T
    gated_t = (go[...].astype(F32) * conv).T.astype(BF16)
    grad_ow = mm(gated_t, og[...])
    gp = jnp.concatenate(
        [
            (gg[...].astype(F32) * conv).astype(BF16),
            (gm * v[...].astype(F32)).astype(BF16),
            (gm * gi[...].astype(F32)).astype(BF16),
        ],
        axis=1,
    )
    gtok[...] = mm(gp, wi[...], NT).astype(BF16)
    grad_iw = mm(tok[...].astype(F32).T.astype(BF16), gp)
    for rt in range(16):
        for cb in range(8):
            src = grad_iw if cb < 6 else grad_ow
            at = 128 * (cb if cb < 6 else cb - 6)
            slab[rt * 8 + cb, 0:16, :] = src[16 * rt : 16 * rt + 16, at : at + 128].astype(BF16)

    gf_pair = jnp.concatenate(
        [scr[:, 8 + ch, :] + scr[:, 10 + ch, :] for ch in range(2)], axis=0
    )
    tmp[...] = gf_pair.T
    gf = tmp[pl.ds(pl.multiple_of((own % 2) * 64, 64), 64), :]
    gk = gf * modulation(dr[...], first, (64, 256))
    grad_fw = mm_full(act2[...].T, gk)
    ga2 = mm_full(gk, fw[...], NT)
    cos2 = jnp.cos(sf[1:2, :] * pre2[...])
    gp2 = ga2 * sf[1:2, :] * cos2
    grad_f2 = jnp.sum(ga2 * pre2[...] * cos2, axis=0, keepdims=True)
    grad_hb = jnp.sum(gp2, axis=0, keepdims=True)
    grad_hw = mm_full(act1[...].T, gp2)
    ga1 = mm_full(gp2, hw[...], NT)
    cos1 = jnp.cos(sf[0:1, :] * pre1[...])
    gp1 = ga1 * sf[0:1, :] * cos1
    grad_f1 = jnp.sum(ga1 * pre1[...] * cos1, axis=0, keepdims=True)
    grad_eb = jnp.sum(gp1, axis=0, keepdims=True)
    sm[...] = jnp.zeros((128, 128), F32)
    sm[0:64, 0:64] = grad_hw
    for k in range(5):
        sm[64 + k : 65 + k, 0:64] = jnp.sum(emb[k] * gp1, axis=0, keepdims=True)
    sm[69:70, 0:64] = grad_eb
    sm[70:71, 0:64] = grad_hb
    sm[71:72, 0:64] = grad_f1
    sm[72:73, 0:64] = grad_f2
    sm[73:74, :] = bias[:, 0:128]
    sm[74:75, :] = bias[:, 128:256]
    small = (jnp.concatenate([grad_fw[:, 0:128], grad_fw[:, 128:256]], axis=0), sm[...])
    for k in range(2):
        hi = small[k].astype(BF16).astype(F32)
        ssc[:, 2 * k, :] = hi
        ssc[:, 2 * k + 1, :] = small[k] - hi
        ssc[:, 4 + 2 * k, :] = jnp.zeros((128, 128), F32)
        ssc[:, 5 + 2 * k, :] = jnp.zeros((128, 128), F32)
    slab[:, 16:24, :] = ssc[...].astype(BF16)


def sum_kernel(recv, out):
    total = jnp.sum(recv[...].astype(F32), axis=0)
    main = total[0:16, :]
    small = total[16:24, :]
    rows = []
    for k in range(2):
        now = small[2 * k : 2 * k + 1, :] + small[2 * k + 1 : 2 * k + 2, :]
        hi = now.astype(BF16).astype(F32)
        rows += [hi, now - hi]
    rows.append(jnp.zeros((4, 128), F32))
    done = jnp.concatenate([main] + rows, axis=0).astype(BF16)
    out[...] = jnp.broadcast_to(done[None], out.shape)


def unpack_kernel(recv, giw, gow, gsb, gew, geb, ghw, ghb, gfw, gsf, scr):
    scale = 1.0 / math.sqrt(4 * LENGTH)
    fscale = scale / 4.0
    for rt in range(16):
        for cb in range(8):
            tile = recv[rt * 8 + cb, 0:16, :].astype(F32) * scale
            if cb < 6:
                giw[16 * rt : 16 * rt + 16, 128 * cb : 128 * cb + 128] = tile
            else:
                gow[16 * rt : 16 * rt + 16, 128 * (cb - 6) : 128 * (cb - 6) + 128] = tile
    scr[...] = recv[:, 16:24, :].astype(F32)
    first = (scr[:, 0, :] + scr[:, 1, :]) * fscale
    gfw[:, 0:128] = first[0:64, :]
    gfw[:, 128:256] = first[64:128, :]
    second = scr[:, 2, :] + scr[:, 3, :]
    ghw[...] = second[0:64, 0:64] * fscale
    gew[...] = second[64:69, 0:64] * fscale
    geb[...] = second[69:70, 0:64] * fscale
    ghb[...] = second[70:71, 0:64] * fscale
    gsf[...] = second[71:73, 0:64] * fscale
    gsb[:, 0:128] = second[73:74, :] * scale
    gsb[:, 128:256] = second[74:75, :] * scale


def call(kernel, name, out_shape, scratch=(), smem_at=()):
    def run(*args):
        return pl.pallas_call(
            kernel,
            out_shape=out_shape,
            in_specs=[
                pl.BlockSpec(memory_space=pltpu.SMEM if k in smem_at else pltpu.VMEM)
                for k in range(len(args))
            ],
            scratch_shapes=list(scratch),
            compiler_params=pltpu.CompilerParams(vmem_limit_bytes=48 * 1024 * 1024),
            name=name,
        )(*args)

    return run


def exchange(x):
    return lax.all_to_all(x, AXES, split_axis=0, concat_axis=0, tiled=True)


def sds(*shape, dtype=F32):
    return jax.ShapeDtypeStruct(shape, dtype)


def shards(
    tokens, out_grad, in_weight, out_weight, skip_bias, embed_weight, embed_bias,
    hidden_weight, hidden_bias, filter_weight, sine_freq, decay_rate,
):
    tok = tokens[0]
    og = out_grad[0]
    decay = decay_rate[None, :]
    square = sds(256, 256, dtype=BF16)
    hidden = sds(64, 64)
    (slab, go, gi, v, gg, bias, emb, pre1, act1, pre2, act2) = call(
        forward_kernel,
        "forward",
        (sds(128, 16, 128, dtype=BF16), square, square, square, square, sds(1, 256),
         sds(5, 64, 64), hidden, hidden, hidden, hidden),
        [pltpu.VMEM((128, 16, 128), F32)],
    )(tok, og, in_weight, out_weight, embed_weight, embed_bias[None, :], hidden_weight,
      hidden_bias[None, :], filter_weight, sine_freq, decay)
    recv = exchange(slab)
    sent = call(
        conv_kernel,
        "conv",
        sds(128, 16, 128, dtype=BF16),
        [
            pltpu.VMEM((128, 16, 128), F32),
            pltpu.VMEM((128, 16, 128), F32),
            pltpu.VMEM((512, 256), BF16),
            pltpu.VMEM((512, 256), BF16),
            pltpu.VMEM((256, 256), F32),
            pltpu.VMEM((256, 256), F32),
            pltpu.VMEM((288, 128), F32),
            pltpu.VMEM((8, 256, 128), BF16),
            pltpu.VMEM((520, 128), F32),
        ],
        (1,),
    )(recv, skip_bias)
    recv = exchange(sent)
    gtok, slab = call(
        backward_kernel,
        "backward",
        (square, sds(128, 24, 128, dtype=BF16)),
        [
            pltpu.VMEM((128, 16, 128), F32),
            pltpu.VMEM((128, 256), F32),
            pltpu.VMEM((128, 128), F32),
            pltpu.VMEM((128, 8, 128), F32),
        ],
    )(recv, go, gi, v, gg, tok, og, in_weight, emb, pre1, act1, pre2, act2, bias, hidden_weight,
      filter_weight, sine_freq, decay)
    recv = exchange(slab)
    total = call(sum_kernel, "total", sds(128, 24, 128, dtype=BF16))(recv)
    recv = exchange(total)
    giw, gow, gsb, gew, geb, ghw, ghb, gfw, gsf = call(
        unpack_kernel,
        "unpack",
        (sds(256, 768), sds(256, 256), sds(1, 256), sds(5, 64), sds(1, 64), sds(64, 64),
         sds(1, 64), sds(64, 256), sds(2, 64)),
        [pltpu.VMEM((128, 8, 128), F32)],
    )(recv)
    return (gtok[None], giw, gow, gsb[0], gew, geb[0], ghw, ghb[0], gfw, gsf)


def solution(mesh):
    return jax.shard_map(
        shards,
        mesh=mesh,
        in_specs=(P("batch", "seq", None),) * 2 + (P(),) * 10,
        out_specs=(P("batch", "seq", None),) + (P(),) * 9,
        check_vma=False,
    )
```

```python
import math

import jax
import jax.numpy as jnp
from jax import lax
from jax.experimental import pallas as pl
from jax.experimental.pallas import tpu as pltpu
from jax.sharding import PartitionSpec as P

F32 = jnp.float32
BF16 = jnp.bfloat16
HIGHEST = lax.Precision.HIGHEST
AXES = ("seq", "batch")
LENGTH = 8192
BANDS = 2
NN = (((1,), (0,)), ((), ()))
NT = (((1,), (1,)), ((), ()))


def mm(a, b, dims=NN):
    return lax.dot_general(a, b, dims, preferred_element_type=F32)


def mm_full(a, b, dims=NN):
    return lax.dot_general(a, b, dims, precision=HIGHEST, preferred_element_type=F32)


def iota(shape, dim):
    return lax.broadcasted_iota(jnp.int32, shape, dim)


def one_hot(cond):
    return jnp.where(cond, 1.0, 0.0).astype(BF16)


def own_index():
    return lax.axis_index("seq") * lax.axis_size("batch") + lax.axis_index("batch")


def modulation(decay, first, shape):
    pos = (first + iota(shape, 0)).astype(F32)
    return 4.0 * jnp.exp(-decay * pos) / math.sqrt(LENGTH)


def forward_kernel(
    tok_h, og_h, wi_h, wo_h, ew_h, eb_h, hw_h, hb_h, fw_h, sf_h, dr_h,
    slab, go_o, gi_o, v_o, gg_o, bias_o, emb_o, pre1_o, act1_o, pre2_o, act2_o,
    tok, og, wi, wo, ew, eb, hw, hb, fw, sf, dr, scr, sems,
):
    pairs = (
        (tok_h, tok), (wi_h, wi), (og_h, og), (wo_h, wo), (sf_h, sf), (ew_h, ew), (eb_h, eb),
        (hw_h, hw), (hb_h, hb), (fw_h, fw), (dr_h, dr),
    )
    copies = [pltpu.make_async_copy(a, b, sems.at[k]) for k, (a, b) in enumerate(pairs)]
    for c in copies:
        c.start()
    first = own_index() * 64
    scaled = (first + iota((64, 64), 0)).astype(F32) / LENGTH
    rows = [scaled]
    for band in range(1, BANDS + 1):
        angle = 2.0 * math.pi * band * scaled
        rows.append(jnp.cos(angle))
        rows.append(jnp.sin(angle))
    for c in copies:
        c.wait()
    proj = mm(tok[...], wi[...])
    go = proj[:, :256].astype(BF16)
    gi = proj[:, 256:512].astype(BF16)
    v = proj[:, 512:].astype(BF16)
    gg = mm(og[...], wo[...], NT).astype(BF16)
    go_o[...] = go
    gi_o[...] = gi
    v_o[...] = v
    gg_o[...] = gg
    mixed = (v.astype(F32) * gi.astype(F32)).astype(BF16).astype(F32)
    gc = (gg.astype(F32) * go.astype(F32)).astype(BF16).astype(F32)
    bias_o[...] = jnp.sum(gc * mixed, axis=0, keepdims=True)
    mixed_t = mixed.T
    gc_t = gc.T
    pre1 = eb[...]
    for k in range(5):
        pre1 = pre1 + rows[k] * ew[k : k + 1, :]
        emb_o[k] = rows[k]
    act1 = jnp.sin(sf[0:1, :] * pre1)
    pre2 = mm_full(act1, hw[...]) + hb[...]
    act2 = jnp.sin(sf[1:2, :] * pre2)
    pre1_o[...] = pre1
    act1_o[...] = act1
    pre2_o[...] = pre2
    act2_o[...] = act2
    filt = mm_full(act2, fw[...]) * modulation(dr[...], first, (64, 256))
    side = 64 * (lax.axis_index("batch") % 2)
    place = one_hot(iota((64, 128), 1) == iota((64, 128), 0) + side)
    filt_t = mm(filt.T.astype(BF16), place)
    for ch in range(2):
        scr[pl.ds(8 + ch, 128, stride=10), :] = filt_t[128 * ch : 128 * ch + 128, :]
        for at, whole in ((0, mixed_t), (4, gc_t)):
            for half in range(2):
                scr[pl.ds(at + 2 * ch + half, 128, stride=10), :] = whole[
                    128 * ch : 128 * ch + 128, 128 * half : 128 * half + 128
                ]
    slab[...] = scr[...].astype(BF16)


def row_rolls(x):
    row = iota(x.shape, 0)
    for bit in range(3):
        x = jnp.where((row >> bit) & 1 == 1, pltpu.roll(x, 1 << bit, 1), x)
    return x


def conv_kernel(recv, skip, out, scr, osc, fscr, ubuf, gpad, gs, gsc):
    scr[...] = recv[...].astype(F32)
    own = own_index()
    row, col = iota((256, 256), 0), iota((256, 256), 1)
    rev256 = one_hot(row + col == 255)
    rev128 = one_hot(iota((128, 128), 0) + iota((128, 128), 1) == 127)

    def source(r):
        blk, sig = r >> 3, r & 7
        return jnp.where(sig < 4, blk * 4 + sig, 128 + (31 - blk) * 4 + sig - 4)

    perm = one_hot(source(row) == col)
    back = one_hot(source(col) == row)
    gather = [
        one_hot(iota((256, 128), 1) >> 1 == 2 * (iota((256, 128), 0) >> 3) + h) for h in range(2)
    ]
    spread_g = one_hot(iota((128, 64), 0) >> 1 == iota((128, 64), 1))
    lane, sub = iota((8, 128), 1), iota((8, 128), 0)
    ready = lane >= sub

    def line(r):
        return scr[pl.ds(r, 128, stride=10), :]

    for ch in range(2):
        f_in = line(8 + ch).astype(BF16)
        fscr[ch, 0:8, :] = jnp.zeros((8, 256), F32)
        for h in range(2):
            fscr[ch, 8:264, 128 * h : 128 * h + 128] = row_rolls(mm(gather[h], f_in))
        ubuf[ch, 0:128, :] = jnp.zeros((128, 128), BF16)

    def toeplitz_step(n, carry):
        for ch in range(2):
            at = pl.multiple_of(8 * n, 8)
            before = fscr[ch, pl.ds(at, 8), 128:256]
            now = fscr[ch, pl.ds(pl.multiple_of(at + 8, 8), 8), :]
            for odd in range(2):
                last = before if odd == 0 else now[:, 0:128]
                this = now[:, 128 * odd : 128 * odd + 128]
                fresh = jnp.where(ready, this, last)
                tiles = [fresh]
                for g in range(1, 16):
                    picked = jnp.where(lane < 128 - 8 * g, fresh, last)
                    tiles.append(pltpu.roll(picked, 8 * g, 1))
                to = pl.multiple_of(256 * n + 128 * (odd + 1), 128)
                ubuf[ch, pl.ds(to, 128), :] = jnp.concatenate(tiles, axis=0).astype(BF16)
        return carry

    lax.fori_loop(0, 32, toeplitz_step, 0)

    for ch in range(2):
        xs = [line(2 * ch + h) for h in range(2)]
        gs_in = [line(4 + 2 * ch + h) for h in range(2)]
        x2 = jnp.concatenate(xs, axis=1).astype(BF16)
        g2 = jnp.concatenate(gs_in, axis=1).astype(BF16)
        g_rev = mm(g2, rev256).astype(BF16)
        mixed_up = mm(perm, jnp.concatenate([x2, g_rev], axis=0))
        shifted = (
            mixed_up.astype(BF16),
            jnp.concatenate([jnp.zeros((8, 256), F32), mixed_up[0:248, :]], axis=0).astype(BF16),
        )
        total = None
        for q in range(4):
            low = 64 * q
            left, right = [], []
            for k in range(8 * q, 8 * q + 8):
                down = 16 * (k // 2)
                piece = shifted[k % 2]
                if down <= low:
                    left.append(piece[low - down : 256 - down, :])
                else:
                    left.append(
                        jnp.concatenate(
                            [jnp.zeros((down - low, 256), BF16), piece[0 : 256 - down, :]], axis=0
                        )
                    )
                u = [ubuf[ch, 128 * n : 128 * n + 128, :] for n in range(2 * k, 2 * k + 3)]
                right.append(jnp.concatenate([u[1], u[2]], axis=1))
                right.append(jnp.concatenate([u[0], u[1]], axis=1))
            part = mm(jnp.concatenate(left, axis=1), jnp.concatenate(right, axis=0))
            if total is None:
                total = part
            else:
                total = jnp.concatenate([total[0:low, :], total[low:, :] + part], axis=0)
        mine = iota((1, 256), 1) == own + 128 * ch
        skip_now = jnp.sum(jnp.where(mine, skip[...], 0.0), axis=1, keepdims=True)
        done = (total + skip_now * mixed_up).astype(BF16)
        apart = mm(back, done)
        conv2 = apart[0:128, :]
        gm2 = mm(apart[128:256, :].astype(BF16), rev256)
        for h in range(2):
            osc[pl.ds(2 * ch + h, 128, stride=10), :] = conv2[:, 128 * h : 128 * h + 128]
            osc[pl.ds(4 + 2 * ch + h, 128, stride=10), :] = gm2[:, 128 * h : 128 * h + 128]

        x_rev = jnp.concatenate(
            [mm(rev128, x.astype(BF16), NT).astype(BF16) for x in xs], axis=1
        )
        for h in range(2):
            gpad[0:128, :] = gs_in[h]
            gpad[128:288, :] = jnp.zeros((160, 128), F32)
            for s in range(4):
                gs[4 * h + s] = gpad[4 * s : 4 * s + 256, :].astype(BF16)

        def corr_step(q, c_last):
            for s in range(4):
                at = pl.multiple_of(16 * q, 16)
                at_next = pl.multiple_of(16 * q + 16 * (s // 3), 16)
                g0 = gs[s, pl.ds(at, 128), :]
                g1 = gs[4 + s, pl.ds(at, 128), :]
                g0_next = gs[(s + 1) % 4, pl.ds(at_next, 128), :]
                right = jnp.concatenate(
                    [
                        jnp.concatenate([g0, g1], axis=1),
                        jnp.concatenate([g1, g0_next], axis=1),
                    ],
                    axis=0,
                )
                both = mm(x_rev, right)
                for odd in range(2):
                    c = both[:, 128 * odd : 128 * odd + 128]
                    part = diagonals(c_last, c)
                    gsc[pl.ds(pl.multiple_of(64 * q + 8 * (2 * s + odd), 8), 8), :] = part
                    c_last = c
            return c_last

        def diagonals(c_last, c):
            part = None
            for g in range(16):
                old = c_last[8 * g : 8 * g + 8, :]
                if c is None:
                    new = jnp.zeros((8, 128), F32)
                else:
                    new = c[8 * g : 8 * g + 8, :]
                now = pltpu.roll(jnp.where(lane + sub >= 127 - 8 * g, old, new), 8 * g + 1, 1)
                part = now if part is None else part + now
            return part

        c_end = lax.fori_loop(0, 8, corr_step, jnp.zeros((128, 128), F32))
        gsc[512:520, :] = diagonals(c_end, None)
        gf = row_rolls(gsc[8:520, :]).reshape(64, 8, 128).sum(axis=1)
        osc[pl.ds(8 + ch, 128, stride=10), :] = mm(spread_g, gf.astype(BF16))
    out[...] = osc[...].astype(BF16)


def backward_kernel(
    recv, go, gi, v, gg, tok, og, wi, emb, pre1, act1, pre2, act2, bias, hw, fw, sf, dr,
    gtok, slab, scr, tmp, sm, ssc,
):
    own = own_index()
    first = own * 64
    scr[...] = recv[...].astype(F32)

    def line(r):
        return scr[pl.ds(r, 128, stride=10), :]

    def whole(at):
        return jnp.concatenate(
            [
                jnp.concatenate([line(at + 2 * ch), line(at + 2 * ch + 1)], axis=1)
                for ch in range(2)
            ],
            axis=0,
        )

    conv = whole(0).T
    gm = whole(4).T
    gated_t = (go[...].astype(F32) * conv).T.astype(BF16)
    grad_ow = mm(gated_t, og[...])
    gp = jnp.concatenate(
        [
            (gg[...].astype(F32) * conv).astype(BF16),
            (gm * v[...].astype(F32)).astype(BF16),
            (gm * gi[...].astype(F32)).astype(BF16),
        ],
        axis=1,
    )
    gtok[...] = mm(gp, wi[...], NT).astype(BF16)
    grad_iw = mm(tok[...].astype(F32).T.astype(BF16), gp)
    for rb in range(2):
        for cb in range(8):
            src = grad_iw if cb < 6 else grad_ow
            at = 128 * (cb if cb < 6 else cb - 6)
            ssc[pl.ds(8 * rb + cb, 128, stride=18), :] = src[
                128 * rb : 128 * rb + 128, at : at + 128
            ]

    tmp[...] = jnp.concatenate([line(8), line(9)], axis=0).T
    gf = tmp[pl.ds(pl.multiple_of((own % 2) * 64, 64), 64), :]
    gk = gf * modulation(dr[...], first, (64, 256))
    grad_fw = mm_full(act2[...].T, gk)
    ga2 = mm_full(gk, fw[...], NT)
    cos2 = jnp.cos(sf[1:2, :] * pre2[...])
    gp2 = ga2 * sf[1:2, :] * cos2
    grad_f2 = jnp.sum(ga2 * pre2[...] * cos2, axis=0, keepdims=True)
    grad_hb = jnp.sum(gp2, axis=0, keepdims=True)
    grad_hw = mm_full(act1[...].T, gp2)
    ga1 = mm_full(gp2, hw[...], NT)
    cos1 = jnp.cos(sf[0:1, :] * pre1[...])
    gp1 = ga1 * sf[0:1, :] * cos1
    grad_f1 = jnp.sum(ga1 * pre1[...] * cos1, axis=0, keepdims=True)
    grad_eb = jnp.sum(gp1, axis=0, keepdims=True)
    sm[...] = jnp.zeros((128, 128), F32)
    sm[0:64, 0:64] = grad_hw
    for k in range(5):
        sm[64 + k : 65 + k, 0:64] = jnp.sum(emb[k] * gp1, axis=0, keepdims=True)
    sm[69:70, 0:64] = grad_eb
    sm[70:71, 0:64] = grad_hb
    sm[71:72, 0:64] = grad_f1
    sm[72:73, 0:64] = grad_f2
    sm[73:74, :] = bias[:, 0:128]
    sm[74:75, :] = bias[:, 128:256]
    ssc[pl.ds(16, 64, stride=18), :] = grad_fw[:, 0:128]
    ssc[pl.ds(16 + 64 * 18, 64, stride=18), :] = grad_fw[:, 128:256]
    ssc[pl.ds(17, 128, stride=18), :] = sm[...]
    slab[...] = ssc[...].astype(BF16)


def mod18(x):
    return x - 18 * jnp.floor((x.astype(F32) + 0.5) / 18.0).astype(jnp.int32)


def sum_kernel(recv, out):
    pick = one_hot(mod18(iota((32, 2304), 1)) == iota((32, 2304), 0))
    total = mm(pick, recv[...]).astype(BF16)
    again = one_hot(mod18(iota((144, 32), 0)) == iota((144, 32), 1))
    block = mm(again, total).astype(BF16)
    for k in range(16):
        out[144 * k : 144 * k + 144, :] = block


def unpack_kernel(recv, giw, gow, gsb, gew, geb, ghw, ghb, gfw, gsf, scr):
    scale = 1.0 / math.sqrt(4 * LENGTH)
    fscale = scale / 4.0
    scr[...] = recv[...].astype(F32)
    for rb in range(2):
        for cb in range(8):
            tile = scr[pl.ds(8 * rb + cb, 128, stride=18), :] * scale
            if cb < 6:
                giw[128 * rb : 128 * rb + 128, 128 * cb : 128 * cb + 128] = tile
            else:
                gow[128 * rb : 128 * rb + 128, 128 * (cb - 6) : 128 * (cb - 6) + 128] = tile
    first = scr[pl.ds(16, 128, stride=18), :] * fscale
    gfw[:, 0:128] = first[0:64, :]
    gfw[:, 128:256] = first[64:128, :]
    second = scr[pl.ds(17, 128, stride=18), :]
    ghw[...] = second[0:64, 0:64] * fscale
    gew[...] = second[64:69, 0:64] * fscale
    geb[...] = second[69:70, 0:64] * fscale
    ghb[...] = second[70:71, 0:64] * fscale
    gsf[...] = second[71:73, 0:64] * fscale
    gsb[:, 0:128] = second[73:74, :] * scale
    gsb[:, 128:256] = second[74:75, :] * scale


def call(kernel, name, out_shape, scratch=(), from_hbm=False):
    def run(*args):
        return pl.pallas_call(
            kernel,
            out_shape=out_shape,
            in_specs=[
                pl.BlockSpec(memory_space=pltpu.HBM if from_hbm else pltpu.VMEM)
                for _ in args
            ],
            scratch_shapes=list(scratch),
            compiler_params=pltpu.CompilerParams(vmem_limit_bytes=48 * 1024 * 1024),
            name=name,
        )(*args)

    return run


def exchange(x, rows):
    y = x.reshape(128, rows // 2, 2, 128)
    y = lax.all_to_all(y, AXES, split_axis=0, concat_axis=0, tiled=True)
    return y.reshape(128 * rows, 128)


def sds(*shape, dtype=F32):
    return jax.ShapeDtypeStruct(shape, dtype)


def shards(
    tokens, out_grad, in_weight, out_weight, skip_bias, embed_weight, embed_bias,
    hidden_weight, hidden_bias, filter_weight, sine_freq, decay_rate,
):
    tok = tokens[0]
    og = out_grad[0]
    decay = decay_rate[None, :]
    square = sds(256, 256, dtype=BF16)
    hidden = sds(64, 64)
    inputs = (tok, og, in_weight, out_weight, embed_weight, embed_bias[None, :], hidden_weight,
              hidden_bias[None, :], filter_weight, sine_freq, decay)
    (slab, go, gi, v, gg, bias, emb, pre1, act1, pre2, act2) = call(
        forward_kernel,
        "forward",
        (sds(1280, 128, dtype=BF16), square, square, square, square, sds(1, 256),
         sds(5, 64, 64), hidden, hidden, hidden, hidden),
        [pltpu.VMEM(x.shape, x.dtype) for x in inputs]
        + [pltpu.VMEM((1280, 128), F32), pltpu.SemaphoreType.DMA((len(inputs),))],
        from_hbm=True,
    )(*inputs)
    recv = exchange(slab, 10)
    sent = call(
        conv_kernel,
        "conv",
        sds(1280, 128, dtype=BF16),
        [
            pltpu.VMEM((1280, 128), F32),
            pltpu.VMEM((1280, 128), F32),
            pltpu.VMEM((2, 264, 256), F32),
            pltpu.VMEM((2, 65 * 128, 128), BF16),
            pltpu.VMEM((288, 128), F32),
            pltpu.VMEM((8, 256, 128), BF16),
            pltpu.VMEM((520, 128), F32),
        ],
    )(recv, skip_bias[None, :])
    recv = exchange(sent, 10)
    gtok, slab = call(
        backward_kernel,
        "backward",
        (square, sds(2304, 128, dtype=BF16)),
        [
            pltpu.VMEM((1280, 128), F32),
            pltpu.VMEM((128, 256), F32),
            pltpu.VMEM((128, 128), F32),
            pltpu.VMEM((2304, 128), F32),
        ],
    )(recv, go, gi, v, gg, tok, og, in_weight, emb, pre1, act1, pre2, act2, bias, hidden_weight,
      filter_weight, sine_freq, decay)
    recv = exchange(slab, 18)
    total = call(sum_kernel, "total", sds(2304, 128, dtype=BF16))(recv)
    recv = exchange(total, 18)
    giw, gow, gsb, gew, geb, ghw, ghb, gfw, gsf = call(
        unpack_kernel,
        "unpack",
        (sds(256, 768), sds(256, 256), sds(1, 256), sds(5, 64), sds(1, 64), sds(64, 64),
         sds(1, 64), sds(64, 256), sds(2, 64)),
        [pltpu.VMEM((2304, 128), F32)],
    )(recv)
    return (gtok[None], giw, gow, gsb[0], gew, geb[0], ghw, ghb[0], gfw, gsf)


def solution(mesh):
    return jax.shard_map(
        shards,
        mesh=mesh,
        in_specs=(P("batch", "seq", None),) * 2 + (P(),) * 10,
        out_specs=(P("batch", "seq", None),) + (P(),) * 9,
        check_vma=False,
    )
```

```python
import math

import jax
import jax.numpy as jnp
from jax import lax
from jax.experimental import pallas as pl
from jax.experimental.pallas import tpu as pltpu
from jax.sharding import PartitionSpec as P

F32 = jnp.float32
BF16 = jnp.bfloat16
HIGHEST = lax.Precision.HIGHEST
AXES = ("seq", "batch")
LENGTH = 8192
BANDS = 2
NN = (((1,), (0,)), ((), ()))
NT = (((1,), (1,)), ((), ()))


def mm(a, b, dims=NN):
    return lax.dot_general(a, b, dims, preferred_element_type=F32)


def mm_full(a, b, dims=NN):
    return lax.dot_general(a, b, dims, precision=HIGHEST, preferred_element_type=F32)


def iota(shape, dim):
    return lax.broadcasted_iota(jnp.int32, shape, dim)


def one_hot(cond):
    return jnp.where(cond, 1.0, 0.0).astype(BF16)


def own_index():
    return lax.axis_index("seq") * lax.axis_size("batch") + lax.axis_index("batch")


def modulation(decay, first, shape):
    pos = (first + iota(shape, 0)).astype(F32)
    return 4.0 * jnp.exp(-decay * pos) / math.sqrt(LENGTH)


def forward_kernel(
    tok_h, og_h, wi_h, wo_h, ew_h, eb_h, hw_h, hb_h, fw_h, sf_h, dr_h, sk_h,
    slab, go_o, gi_o, v_o, gg_o, bias_o, emb_o, pre1_o, act1_o, pre2_o, act2_o, sk_o,
    tok, og, wi, wo, ew, eb, hw, hb, fw, sf, dr, sk, scr, sems,
):
    pairs = (
        (tok_h, tok), (wi_h, wi), (og_h, og), (wo_h, wo), (sf_h, sf), (ew_h, ew), (eb_h, eb),
        (hw_h, hw), (hb_h, hb), (fw_h, fw), (dr_h, dr), (sk_h, sk),
    )
    copies = [pltpu.make_async_copy(a, b, sems.at[k]) for k, (a, b) in enumerate(pairs)]
    for c in copies:
        c.start()
    first = own_index() * 64
    scaled = (first + iota((64, 64), 0)).astype(F32) / LENGTH
    rows = [scaled]
    for band in range(1, BANDS + 1):
        angle = 2.0 * math.pi * band * scaled
        rows.append(jnp.cos(angle))
        rows.append(jnp.sin(angle))
    for c in copies:
        c.wait()
    proj = mm(tok[...], wi[...])
    go = proj[:, :256].astype(BF16)
    gi = proj[:, 256:512].astype(BF16)
    v = proj[:, 512:].astype(BF16)
    gg = mm(og[...], wo[...], NT).astype(BF16)
    go_o[...] = go
    gi_o[...] = gi
    v_o[...] = v
    gg_o[...] = gg
    mixed = (v.astype(F32) * gi.astype(F32)).astype(BF16).astype(F32)
    gc = (gg.astype(F32) * go.astype(F32)).astype(BF16).astype(F32)
    sk_o[...] = sk[...]
    bias_o[...] = jnp.sum(gc * mixed, axis=0, keepdims=True)
    mixed_t = mixed.T
    gc_t = gc.T
    pre1 = eb[...]
    for k in range(5):
        pre1 = pre1 + rows[k] * ew[k : k + 1, :]
        emb_o[k] = rows[k]
    act1 = jnp.sin(sf[0:1, :] * pre1)
    pre2 = mm_full(act1, hw[...]) + hb[...]
    act2 = jnp.sin(sf[1:2, :] * pre2)
    pre1_o[...] = pre1
    act1_o[...] = act1
    pre2_o[...] = pre2
    act2_o[...] = act2
    filt = mm_full(act2, fw[...]) * modulation(dr[...], first, (64, 256))
    side = 64 * (lax.axis_index("batch") % 2)
    place = one_hot(iota((64, 128), 1) == iota((64, 128), 0) + side)
    filt_t = mm(filt.T.astype(BF16), place)
    for ch in range(2):
        scr[pl.ds(8 + ch, 128, stride=10), :] = filt_t[128 * ch : 128 * ch + 128, :]
        for at, whole in ((0, mixed_t), (4, gc_t)):
            for half in range(2):
                scr[pl.ds(at + 2 * ch + half, 128, stride=10), :] = whole[
                    128 * ch : 128 * ch + 128, 128 * half : 128 * half + 128
                ]
    slab[...] = scr[...].astype(BF16)


def row_rolls(x, bits):
    row = iota(x.shape, 0)
    for bit in range(bits):
        x = jnp.where((row >> bit) & 1 == 1, pltpu.roll(x, 1 << bit, 1), x)
    return x


def conv_kernel(recv, skip, out, scr, osc, fscr, ubuf, gpad, gs, gsc):
    scr[...] = recv[...].astype(F32)
    own = own_index()
    row, col = iota((256, 256), 0), iota((256, 256), 1)
    rev256 = one_hot(row + col == 255)
    rev128 = one_hot(iota((128, 128), 0) + iota((128, 128), 1) == 127)

    def source(r):
        blk, sig = r >> 3, r & 7
        return jnp.where(sig < 4, blk * 4 + sig, 128 + (31 - blk) * 4 + sig - 4)

    perm = one_hot(source(row) == col)
    back = one_hot(source(col) == row)
    gather = [
        one_hot(iota((512, 128), 1) >> 1 == 2 * (iota((512, 128), 0) >> 4) + h) for h in range(2)
    ]
    spread_g = one_hot(iota((128, 64), 0) >> 1 == iota((128, 64), 1))
    lane, sub = iota((8, 128), 1), iota((8, 128), 0)
    lane16, sub16 = iota((16, 128), 1), iota((16, 128), 0)

    def line(r):
        return scr[pl.ds(r, 128, stride=10), :]

    mixed_up, shifted, x_revs = [], [], []
    for ch in range(2):
        f_in = line(8 + ch).astype(BF16)
        fscr[ch, 0:16, :] = jnp.zeros((16, 256), BF16)
        for h in range(2):
            fscr[ch, 16:528, 128 * h : 128 * h + 128] = row_rolls(mm(gather[h], f_in), 4).astype(BF16)
        ubuf[ch, 0:128, :] = jnp.zeros((128, 128), BF16)
    for ch in range(2):
        xs = [line(2 * ch + h) for h in range(2)]
        gs_in = [line(4 + 2 * ch + h) for h in range(2)]
        x2 = jnp.concatenate(xs, axis=1).astype(BF16)
        g2 = jnp.concatenate(gs_in, axis=1).astype(BF16)
        g_rev = mm(g2, rev256).astype(BF16)
        up = mm(perm, jnp.concatenate([x2, g_rev], axis=0))
        mixed_up.append(up)
        shifted.append(
            (
                up.astype(BF16),
                jnp.concatenate([jnp.zeros((8, 256), F32), up[0:248, :]], axis=0).astype(BF16),
            )
        )
        x_revs.append(
            jnp.concatenate([mm(rev128, x.astype(BF16), NT).astype(BF16) for x in xs], axis=1)
        )
        for h in range(2):
            at = 2 * ch + h
            gpad[at, 0:128, :] = gs_in[h]
            gpad[at, 128:288, :] = jnp.zeros((160, 128), F32)
            for s in range(4):
                gs[4 * at + s] = gpad[at, 4 * s : 4 * s + 256, :].astype(BF16)

    def diagonals(c_last, c):
        part = None
        for g in range(16):
            old = c_last[8 * g : 8 * g + 8, :]
            new = jnp.zeros((8, 128), F32) if c is None else c[8 * g : 8 * g + 8, :]
            now = pltpu.roll(jnp.where(lane + sub >= 127 - 8 * g, old, new), 8 * g + 1, 1)
            part = now if part is None else part + now
        return part

    def step(q, carry):
        ends = []
        for ch in range(2):
            for k in range(4):
                at = pl.multiple_of(64 * q + 16 * k, 16)
                before = fscr[ch, pl.ds(at, 16), 128:256]
                now = fscr[ch, pl.ds(pl.multiple_of(at + 16, 16), 16), :]
                for odd in range(2):
                    last = before if odd == 0 else now[:, 0:128]
                    this = now[:, 128 * odd : 128 * odd + 128]
                    fresh = jnp.where(lane16 >= sub16, this, last)
                    tiles = [fresh]
                    for g in range(1, 8):
                        picked = jnp.where(lane16 < 128 - 16 * g, fresh, last)
                        tiles.append(pltpu.roll(picked, 16 * g, 1))
                    to = pl.multiple_of(1024 * q + 256 * k + 128 * (odd + 1), 128)
                    ubuf[ch, pl.ds(to, 128), :] = jnp.concatenate(tiles, axis=0)
            c_last = carry[ch]
            for s in range(4):
                at = pl.multiple_of(16 * q, 16)
                at_next = pl.multiple_of(16 * q + 16 * (s // 3), 16)
                g0 = gs[8 * ch + s, pl.ds(at, 128), :]
                g1 = gs[8 * ch + 4 + s, pl.ds(at, 128), :]
                g0_next = gs[8 * ch + (s + 1) % 4, pl.ds(at_next, 128), :]
                right = jnp.concatenate(
                    [
                        jnp.concatenate([g0, g1], axis=1),
                        jnp.concatenate([g1, g0_next], axis=1),
                    ],
                    axis=0,
                )
                both = mm(x_revs[ch], right)
                for odd in range(2):
                    c = both[:, 128 * odd : 128 * odd + 128]
                    to = pl.multiple_of(64 * q + 8 * (2 * s + odd), 8)
                    gsc[ch, pl.ds(to, 8), :] = diagonals(c_last, c)
                    c_last = c
            ends.append(c_last)
        return tuple(ends)

    ends = lax.fori_loop(0, 8, step, (jnp.zeros((128, 128), F32),) * 2)

    for ch in range(2):
        total = None
        for q in range(4):
            low = 64 * q
            left, right = [], []
            for k in range(8 * q, 8 * q + 8):
                down = 16 * (k // 2)
                piece = shifted[ch][k % 2]
                if down <= low:
                    left.append(piece[low - down : 256 - down, :])
                else:
                    left.append(
                        jnp.concatenate(
                            [jnp.zeros((down - low, 256), BF16), piece[0 : 256 - down, :]], axis=0
                        )
                    )
                u = [ubuf[ch, 128 * n : 128 * n + 128, :] for n in range(2 * k, 2 * k + 3)]
                right.append(jnp.concatenate([u[1], u[2]], axis=1))
                right.append(jnp.concatenate([u[0], u[1]], axis=1))
            part = mm(jnp.concatenate(left, axis=1), jnp.concatenate(right, axis=0))
            if total is None:
                total = part
            else:
                total = jnp.concatenate([total[0:low, :], total[low:, :] + part], axis=0)
        mine = iota((1, 256), 1) == own + 128 * ch
        skip_now = jnp.sum(jnp.where(mine, skip[...], 0.0), axis=1, keepdims=True)
        done = (total + skip_now * mixed_up[ch]).astype(BF16)
        apart = mm(back, done)
        conv2 = apart[0:128, :]
        gm2 = mm(apart[128:256, :].astype(BF16), rev256)
        for h in range(2):
            osc[pl.ds(2 * ch + h, 128, stride=10), :] = conv2[:, 128 * h : 128 * h + 128]
            osc[pl.ds(4 + 2 * ch + h, 128, stride=10), :] = gm2[:, 128 * h : 128 * h + 128]
        gsc[ch, 512:520, :] = diagonals(ends[ch], None)
        gf = row_rolls(gsc[ch, 8:520, :], 3).reshape(64, 8, 128).sum(axis=1)
        osc[pl.ds(8 + ch, 128, stride=10), :] = mm(spread_g, gf.astype(BF16))
    out[...] = osc[...].astype(BF16)


def backward_kernel(
    recv, go, gi, v, gg, tok, og, wi, emb, pre1, act1, pre2, act2, bias, hw, fw, sf, dr,
    gtok, slab, scr, tmp, sm, ssc,
):
    own = own_index()
    first = own * 64
    scr[...] = recv[...].astype(F32)

    def line(r):
        return scr[pl.ds(r, 128, stride=10), :]

    def whole(at):
        return jnp.concatenate(
            [
                jnp.concatenate([line(at + 2 * ch), line(at + 2 * ch + 1)], axis=1)
                for ch in range(2)
            ],
            axis=0,
        )

    conv = whole(0).T
    gm = whole(4).T
    gated_t = (go[...].astype(F32) * conv).T.astype(BF16)
    grad_ow = mm(gated_t, og[...])
    gp = jnp.concatenate(
        [
            (gg[...].astype(F32) * conv).astype(BF16),
            (gm * v[...].astype(F32)).astype(BF16),
            (gm * gi[...].astype(F32)).astype(BF16),
        ],
        axis=1,
    )
    gtok[...] = mm(gp, wi[...], NT).astype(BF16)
    grad_iw = mm(tok[...].astype(F32).T.astype(BF16), gp)
    for rb in range(2):
        for cb in range(8):
            src = grad_iw if cb < 6 else grad_ow
            at = 128 * (cb if cb < 6 else cb - 6)
            ssc[pl.ds(8 * rb + cb, 128, stride=18), :] = src[
                128 * rb : 128 * rb + 128, at : at + 128
            ]

    tmp[...] = jnp.concatenate([line(8), line(9)], axis=0).T
    gf = tmp[pl.ds(pl.multiple_of((own % 2) * 64, 64), 64), :]
    gk = gf * modulation(dr[...], first, (64, 256))
    grad_fw = mm_full(act2[...].T, gk)
    ga2 = mm_full(gk, fw[...], NT)
    cos2 = jnp.cos(sf[1:2, :] * pre2[...])
    gp2 = ga2 * sf[1:2, :] * cos2
    grad_f2 = jnp.sum(ga2 * pre2[...] * cos2, axis=0, keepdims=True)
    grad_hb = jnp.sum(gp2, axis=0, keepdims=True)
    grad_hw = mm_full(act1[...].T, gp2)
    ga1 = mm_full(gp2, hw[...], NT)
    cos1 = jnp.cos(sf[0:1, :] * pre1[...])
    gp1 = ga1 * sf[0:1, :] * cos1
    grad_f1 = jnp.sum(ga1 * pre1[...] * cos1, axis=0, keepdims=True)
    grad_eb = jnp.sum(gp1, axis=0, keepdims=True)
    sm[...] = jnp.zeros((128, 128), F32)
    sm[0:64, 0:64] = grad_hw
    for k in range(5):
        sm[64 + k : 65 + k, 0:64] = jnp.sum(emb[k] * gp1, axis=0, keepdims=True)
    sm[69:70, 0:64] = grad_eb
    sm[70:71, 0:64] = grad_hb
    sm[71:72, 0:64] = grad_f1
    sm[72:73, 0:64] = grad_f2
    sm[73:74, :] = bias[:, 0:128]
    sm[74:75, :] = bias[:, 128:256]
    ssc[pl.ds(16, 64, stride=18), :] = grad_fw[:, 0:128]
    ssc[pl.ds(16 + 64 * 18, 64, stride=18), :] = grad_fw[:, 128:256]
    ssc[pl.ds(17, 128, stride=18), :] = sm[...]
    slab[...] = ssc[...].astype(BF16)


def mod18(x):
    return x - 18 * jnp.floor((x.astype(F32) + 0.5) / 18.0).astype(jnp.int32)


def sum_kernel(recv, out):
    pick = one_hot(mod18(iota((32, 2304), 1)) == iota((32, 2304), 0))
    total = mm(pick, recv[...]).astype(BF16)
    again = one_hot(mod18(iota((144, 32), 0)) == iota((144, 32), 1))
    block = mm(again, total).astype(BF16)
    for k in range(16):
        out[144 * k : 144 * k + 144, :] = block


def unpack_kernel(recv, giw, gow, gsb, gew, geb, ghw, ghb, gfw, gsf, scr):
    scale = 1.0 / math.sqrt(4 * LENGTH)
    fscale = scale / 4.0
    scr[...] = recv[...].astype(F32)
    for rb in range(2):
        for cb in range(8):
            tile = scr[pl.ds(8 * rb + cb, 128, stride=18), :] * scale
            if cb < 6:
                giw[128 * rb : 128 * rb + 128, 128 * cb : 128 * cb + 128] = tile
            else:
                gow[128 * rb : 128 * rb + 128, 128 * (cb - 6) : 128 * (cb - 6) + 128] = tile
    first = scr[pl.ds(16, 128, stride=18), :] * fscale
    gfw[:, 0:128] = first[0:64, :]
    gfw[:, 128:256] = first[64:128, :]
    second = scr[pl.ds(17, 128, stride=18), :]
    ghw[...] = second[0:64, 0:64] * fscale
    gew[...] = second[64:69, 0:64] * fscale
    geb[...] = second[69:70, 0:64] * fscale
    ghb[...] = second[70:71, 0:64] * fscale
    gsf[...] = second[71:73, 0:64] * fscale
    gsb[:, 0:128] = second[73:74, :] * scale
    gsb[:, 128:256] = second[74:75, :] * scale


def call(kernel, name, out_shape, scratch=(), from_hbm=False):
    def run(*args):
        return pl.pallas_call(
            kernel,
            out_shape=out_shape,
            in_specs=[
                pl.BlockSpec(memory_space=pltpu.HBM if from_hbm else pltpu.VMEM)
                for _ in args
            ],
            scratch_shapes=list(scratch),
            compiler_params=pltpu.CompilerParams(vmem_limit_bytes=48 * 1024 * 1024),
            name=name,
        )(*args)

    return run


def exchange(x, rows):
    y = x.reshape(128, rows // 2, 2, 128)
    y = lax.all_to_all(y, AXES, split_axis=0, concat_axis=0, tiled=True)
    return y.reshape(128 * rows, 128)


def sds(*shape, dtype=F32):
    return jax.ShapeDtypeStruct(shape, dtype)


def shards(
    tokens, out_grad, in_weight, out_weight, skip_bias, embed_weight, embed_bias,
    hidden_weight, hidden_bias, filter_weight, sine_freq, decay_rate,
):
    tok = tokens[0]
    og = out_grad[0]
    decay = decay_rate[None, :]
    square = sds(256, 256, dtype=BF16)
    hidden = sds(64, 64)
    inputs = (tok, og, in_weight, out_weight, embed_weight, embed_bias[None, :], hidden_weight,
              hidden_bias[None, :], filter_weight, sine_freq, decay, skip_bias[None, :])
    (slab, go, gi, v, gg, bias, emb, pre1, act1, pre2, act2, skip) = call(
        forward_kernel,
        "forward",
        (sds(1280, 128, dtype=BF16), square, square, square, square, sds(1, 256),
         sds(5, 64, 64), hidden, hidden, hidden, hidden, sds(1, 256)),
        [pltpu.VMEM(x.shape, x.dtype) for x in inputs]
        + [pltpu.VMEM((1280, 128), F32), pltpu.SemaphoreType.DMA((len(inputs),))],
        from_hbm=True,
    )(*(pltpu.with_memory_space_constraint(x, pltpu.HBM) for x in inputs))
    recv = exchange(slab, 10)
    sent = call(
        conv_kernel,
        "conv",
        sds(1280, 128, dtype=BF16),
        [
            pltpu.VMEM((1280, 128), F32),
            pltpu.VMEM((1280, 128), F32),
            pltpu.VMEM((2, 528, 256), BF16),
            pltpu.VMEM((2, 65 * 128, 128), BF16),
            pltpu.VMEM((4, 288, 128), F32),
            pltpu.VMEM((16, 256, 128), BF16),
            pltpu.VMEM((2, 520, 128), F32),
        ],
    )(recv, skip)
    recv = exchange(sent, 10)
    gtok, slab = call(
        backward_kernel,
        "backward",
        (square, sds(2304, 128, dtype=BF16)),
        [
            pltpu.VMEM((1280, 128), F32),
            pltpu.VMEM((128, 256), F32),
            pltpu.VMEM((128, 128), F32),
            pltpu.VMEM((2304, 128), F32),
        ],
    )(recv, go, gi, v, gg, tok, og, in_weight, emb, pre1, act1, pre2, act2, bias, hidden_weight,
      filter_weight, sine_freq, decay)
    recv = exchange(slab, 18)
    total = call(sum_kernel, "total", sds(2304, 128, dtype=BF16))(recv)
    recv = exchange(total, 18)
    giw, gow, gsb, gew, geb, ghw, ghb, gfw, gsf = call(
        unpack_kernel,
        "unpack",
        (sds(256, 768), sds(256, 256), sds(1, 256), sds(5, 64), sds(1, 64), sds(64, 64),
         sds(1, 64), sds(64, 256), sds(2, 64)),
        [pltpu.VMEM((2304, 128), F32)],
    )(recv)
    return (gtok[None], giw, gow, gsb[0], gew, geb[0], ghw, ghb[0], gfw, gsf)


def solution(mesh):
    return jax.shard_map(
        shards,
        mesh=mesh,
        in_specs=(P("batch", "seq", None),) * 2 + (P(),) * 10,
        out_specs=(P("batch", "seq", None),) + (P(),) * 9,
        check_vma=False,
    )
```

```python
import math

import jax
import jax.numpy as jnp
from jax import lax
from jax.experimental import pallas as pl
from jax.experimental.pallas import tpu as pltpu
from jax.sharding import PartitionSpec as P

F32 = jnp.float32
BF16 = jnp.bfloat16
HIGHEST = lax.Precision.HIGHEST
AXES = ("seq", "batch")
LENGTH = 8192
BANDS = 2
NN = (((1,), (0,)), ((), ()))
NT = (((1,), (1,)), ((), ()))


def mm(a, b, dims=NN):
    return lax.dot_general(a, b, dims, preferred_element_type=F32)


def mm_full(a, b, dims=NN):
    return lax.dot_general(a, b, dims, precision=HIGHEST, preferred_element_type=F32)


def iota(shape, dim):
    return lax.broadcasted_iota(jnp.int32, shape, dim)


def one_hot(cond):
    return jnp.where(cond, 1.0, 0.0).astype(BF16)


def own_index():
    return lax.axis_index("seq") * lax.axis_size("batch") + lax.axis_index("batch")


def modulation(decay, first, shape):
    pos = (first + iota(shape, 0)).astype(F32)
    return 4.0 * jnp.exp(-decay * pos) / math.sqrt(LENGTH)


def forward_kernel(
    tok_h, og_h, wi_h, wo_h, ew_h, eb_h, hw_h, hb_h, fw_h, sf_h, dr_h, sk_h,
    slab, go_o, gi_o, v_o, gg_o, bias_o, emb_o, pre1_o, act1_o, pre2_o, act2_o,
    sk_o, mod_o, hw_o, fw_o, sf_o,
    tok, og, wi, wo, ew, eb, hw, hb, fw, sf, dr, sk, scr, sems,
):
    pairs = (
        (tok_h, tok), (wi_h, wi), (og_h, og), (wo_h, wo), (sf_h, sf), (ew_h, ew), (eb_h, eb),
        (hw_h, hw), (hb_h, hb), (fw_h, fw), (dr_h, dr), (sk_h, sk),
    )
    copies = [pltpu.make_async_copy(a, b, sems.at[k]) for k, (a, b) in enumerate(pairs)]
    for c in copies:
        c.start()
    first = own_index() * 64
    scaled = (first + iota((64, 64), 0)).astype(F32) / LENGTH
    rows = [scaled]
    for band in range(1, BANDS + 1):
        angle = 2.0 * math.pi * band * scaled
        rows.append(jnp.cos(angle))
        rows.append(jnp.sin(angle))
    for c in copies:
        c.wait()
    proj = mm(tok[...], wi[...])
    go = proj[:, :256].astype(BF16)
    gi = proj[:, 256:512].astype(BF16)
    v = proj[:, 512:].astype(BF16)
    gg = mm(og[...], wo[...], NT).astype(BF16)
    go_o[...] = go
    gi_o[...] = gi
    v_o[...] = v
    gg_o[...] = gg
    mixed = (v.astype(F32) * gi.astype(F32)).astype(BF16).astype(F32)
    gc = (gg.astype(F32) * go.astype(F32)).astype(BF16).astype(F32)
    sk_o[...] = sk[...]
    hw_o[...] = hw[...]
    fw_o[...] = fw[...]
    sf_o[...] = sf[...]
    bias_o[...] = jnp.sum(gc * mixed, axis=0, keepdims=True)
    mixed_t = mixed.T
    gc_t = gc.T
    pre1 = eb[...]
    for k in range(5):
        pre1 = pre1 + rows[k] * ew[k : k + 1, :]
        emb_o[k] = rows[k]
    act1 = jnp.sin(sf[0:1, :] * pre1)
    pre2 = mm_full(act1, hw[...]) + hb[...]
    act2 = jnp.sin(sf[1:2, :] * pre2)
    pre1_o[...] = pre1
    act1_o[...] = act1
    pre2_o[...] = pre2
    act2_o[...] = act2
    modul = modulation(dr[...], first, (64, 256))
    mod_o[...] = modul
    filt = mm_full(act2, fw[...]) * modul
    side = 64 * (lax.axis_index("batch") % 2)
    place = one_hot(iota((64, 128), 1) == iota((64, 128), 0) + side)
    filt_t = mm(filt.T.astype(BF16), place)
    for ch in range(2):
        scr[pl.ds(8 + ch, 128, stride=10), :] = filt_t[128 * ch : 128 * ch + 128, :]
        for at, whole in ((0, mixed_t), (4, gc_t)):
            for half in range(2):
                scr[pl.ds(at + 2 * ch + half, 128, stride=10), :] = whole[
                    128 * ch : 128 * ch + 128, 128 * half : 128 * half + 128
                ]
    slab[...] = scr[...].astype(BF16)


def row_rolls(x, bits):
    row = iota(x.shape, 0)
    for bit in range(bits):
        x = jnp.where((row >> bit) & 1 == 1, pltpu.roll(x, 1 << bit, 1), x)
    return x


def conv_kernel(recv, skip, out, scr, osc, fscr, ubuf, gpad, gs, gsc):
    scr[...] = recv[...].astype(F32)
    own = own_index()
    row, col = iota((256, 256), 0), iota((256, 256), 1)
    rev256 = one_hot(row + col == 255)
    rev128 = one_hot(iota((128, 128), 0) + iota((128, 128), 1) == 127)

    def source(r):
        blk, sig = r >> 3, r & 7
        return jnp.where(sig < 4, blk * 4 + sig, 128 + (31 - blk) * 4 + sig - 4)

    perm = one_hot(source(row) == col)
    back = one_hot(source(col) == row)
    gather = [
        one_hot(iota((512, 128), 1) >> 1 == 2 * (iota((512, 128), 0) >> 4) + h) for h in range(2)
    ]
    spread_g = one_hot(iota((128, 64), 0) >> 1 == iota((128, 64), 1))
    lane, sub = iota((8, 128), 1), iota((8, 128), 0)
    lane16, sub16 = iota((16, 128), 1), iota((16, 128), 0)

    def line(r):
        return scr[pl.ds(r, 128, stride=10), :]

    mixed_up, shifted, x_revs = [], [], []
    for ch in range(2):
        f_in = line(8 + ch).astype(BF16)
        fscr[ch, 0:16, :] = jnp.zeros((16, 256), BF16)
        for h in range(2):
            fscr[ch, 16:528, 128 * h : 128 * h + 128] = row_rolls(mm(gather[h], f_in), 4).astype(BF16)
        ubuf[ch, 0:128, :] = jnp.zeros((128, 128), BF16)
    for ch in range(2):
        xs = [line(2 * ch + h) for h in range(2)]
        gs_in = [line(4 + 2 * ch + h) for h in range(2)]
        x2 = jnp.concatenate(xs, axis=1).astype(BF16)
        g2 = jnp.concatenate(gs_in, axis=1).astype(BF16)
        g_rev = mm(g2, rev256).astype(BF16)
        up = mm(perm, jnp.concatenate([x2, g_rev], axis=0))
        mixed_up.append(up)
        shifted.append(
            (
                up.astype(BF16),
                jnp.concatenate([jnp.zeros((8, 256), F32), up[0:248, :]], axis=0).astype(BF16),
            )
        )
        x_revs.append(
            jnp.concatenate([mm(rev128, x.astype(BF16), NT).astype(BF16) for x in xs], axis=1)
        )
        for h in range(2):
            at = 2 * ch + h
            gpad[at, 0:128, :] = gs_in[h]
            gpad[at, 128:288, :] = jnp.zeros((160, 128), F32)
            for s in range(4):
                gs[4 * at + s] = gpad[at, 4 * s : 4 * s + 256, :].astype(BF16)

    def diagonals(c_last, c):
        part = None
        for g in range(16):
            old = c_last[8 * g : 8 * g + 8, :]
            new = jnp.zeros((8, 128), F32) if c is None else c[8 * g : 8 * g + 8, :]
            now = pltpu.roll(jnp.where(lane + sub >= 127 - 8 * g, old, new), 8 * g + 1, 1)
            part = now if part is None else part + now
        return part

    def step(q, carry):
        ends = []
        for ch in range(2):
            for k in range(4):
                at = pl.multiple_of(64 * q + 16 * k, 16)
                before = fscr[ch, pl.ds(at, 16), 128:256]
                now = fscr[ch, pl.ds(pl.multiple_of(at + 16, 16), 16), :]
                for odd in range(2):
                    last = before if odd == 0 else now[:, 0:128]
                    this = now[:, 128 * odd : 128 * odd + 128]
                    fresh = jnp.where(lane16 >= sub16, this, last)
                    tiles = [fresh]
                    for g in range(1, 8):
                        picked = jnp.where(lane16 < 128 - 16 * g, fresh, last)
                        tiles.append(pltpu.roll(picked, 16 * g, 1))
                    to = pl.multiple_of(1024 * q + 256 * k + 128 * (odd + 1), 128)
                    ubuf[ch, pl.ds(to, 128), :] = jnp.concatenate(tiles, axis=0)
            c_last = carry[ch]
            for s in range(4):
                at = pl.multiple_of(16 * q, 16)
                at_next = pl.multiple_of(16 * q + 16 * (s // 3), 16)
                g0 = gs[8 * ch + s, pl.ds(at, 128), :]
                g1 = gs[8 * ch + 4 + s, pl.ds(at, 128), :]
                g0_next = gs[8 * ch + (s + 1) % 4, pl.ds(at_next, 128), :]
                right = jnp.concatenate(
                    [
                        jnp.concatenate([g0, g1], axis=1),
                        jnp.concatenate([g1, g0_next], axis=1),
                    ],
                    axis=0,
                )
                both = mm(x_revs[ch], right)
                for odd in range(2):
                    c = both[:, 128 * odd : 128 * odd + 128]
                    to = pl.multiple_of(64 * q + 8 * (2 * s + odd), 8)
                    gsc[ch, pl.ds(to, 8), :] = diagonals(c_last, c)
                    c_last = c
            ends.append(c_last)
        return tuple(ends)

    ends = lax.fori_loop(0, 8, step, (jnp.zeros((128, 128), F32),) * 2)

    for ch in range(2):
        total = None
        for q in range(4):
            low = 64 * q
            left, right = [], []
            for k in range(8 * q, 8 * q + 8):
                down = 16 * (k // 2)
                piece = shifted[ch][k % 2]
                if down <= low:
                    left.append(piece[low - down : 256 - down, :])
                else:
                    left.append(
                        jnp.concatenate(
                            [jnp.zeros((down - low, 256), BF16), piece[0 : 256 - down, :]], axis=0
                        )
                    )
                u = [ubuf[ch, 128 * n : 128 * n + 128, :] for n in range(2 * k, 2 * k + 3)]
                right.append(jnp.concatenate([u[1], u[2]], axis=1))
                right.append(jnp.concatenate([u[0], u[1]], axis=1))
            part = mm(jnp.concatenate(left, axis=1), jnp.concatenate(right, axis=0))
            if total is None:
                total = part
            else:
                total = jnp.concatenate([total[0:low, :], total[low:, :] + part], axis=0)
        mine = iota((1, 256), 1) == own + 128 * ch
        skip_now = jnp.sum(jnp.where(mine, skip[...], 0.0), axis=1, keepdims=True)
        done = (total + skip_now * mixed_up[ch]).astype(BF16)
        apart = mm(back, done)
        conv2 = apart[0:128, :]
        gm2 = mm(apart[128:256, :].astype(BF16), rev256)
        for h in range(2):
            osc[pl.ds(2 * ch + h, 128, stride=10), :] = conv2[:, 128 * h : 128 * h + 128]
            osc[pl.ds(4 + 2 * ch + h, 128, stride=10), :] = gm2[:, 128 * h : 128 * h + 128]
        gsc[ch, 512:520, :] = diagonals(ends[ch], None)
        gf = row_rolls(gsc[ch, 8:520, :], 3).reshape(64, 8, 128).sum(axis=1)
        osc[pl.ds(8 + ch, 128, stride=10), :] = mm(spread_g, gf.astype(BF16))
    out[...] = osc[...].astype(BF16)


def backward_kernel(
    recv, go, gi, v, gg, tok, og, wi, emb, pre1, act1, pre2, act2, bias, modul, hw, fw, sf,
    gtok, kept, given, scr, tmp, sm, ssc,
):
    own = own_index()
    scr[...] = recv[...].astype(F32)

    def line(r):
        return scr[pl.ds(r, 128, stride=10), :]

    def whole(at):
        return jnp.concatenate(
            [
                jnp.concatenate([line(at + 2 * ch), line(at + 2 * ch + 1)], axis=1)
                for ch in range(2)
            ],
            axis=0,
        )

    conv = whole(0).T
    gm = whole(4).T
    gated_t = (go[...].astype(F32) * conv).T.astype(BF16)
    grad_ow = mm(gated_t, og[...])
    gp = jnp.concatenate(
        [
            (gg[...].astype(F32) * conv).astype(BF16),
            (gm * v[...].astype(F32)).astype(BF16),
            (gm * gi[...].astype(F32)).astype(BF16),
        ],
        axis=1,
    )
    gtok[...] = mm(gp, wi[...], NT).astype(BF16)
    grad_iw = mm(tok[...].astype(F32).T.astype(BF16), gp)
    for rb in range(2):
        for cb in range(8):
            src = grad_iw if cb < 6 else grad_ow
            at = 128 * (cb if cb < 6 else cb - 6)
            ssc[pl.ds(8 * rb + cb, 128, stride=18), :] = src[
                128 * rb : 128 * rb + 128, at : at + 128
            ]

    tmp[...] = jnp.concatenate([line(8), line(9)], axis=0).T
    gf = tmp[pl.ds(pl.multiple_of((own % 2) * 64, 64), 64), :]
    gk = gf * modul[...]
    grad_fw = mm_full(act2[...].T, gk)
    ga2 = mm_full(gk, fw[...], NT)
    cos2 = jnp.cos(sf[1:2, :] * pre2[...])
    gp2 = ga2 * sf[1:2, :] * cos2
    grad_f2 = jnp.sum(ga2 * pre2[...] * cos2, axis=0, keepdims=True)
    grad_hb = jnp.sum(gp2, axis=0, keepdims=True)
    grad_hw = mm_full(act1[...].T, gp2)
    ga1 = mm_full(gp2, hw[...], NT)
    cos1 = jnp.cos(sf[0:1, :] * pre1[...])
    gp1 = ga1 * sf[0:1, :] * cos1
    grad_f1 = jnp.sum(ga1 * pre1[...] * cos1, axis=0, keepdims=True)
    grad_eb = jnp.sum(gp1, axis=0, keepdims=True)
    sm[...] = jnp.zeros((128, 128), F32)
    sm[0:64, 0:64] = grad_hw
    for k in range(5):
        sm[64 + k : 65 + k, 0:64] = jnp.sum(emb[k] * gp1, axis=0, keepdims=True)
    sm[69:70, 0:64] = grad_eb
    sm[70:71, 0:64] = grad_hb
    sm[71:72, 0:64] = grad_f1
    sm[72:73, 0:64] = grad_f2
    sm[73:74, :] = bias[:, 0:128]
    sm[74:75, :] = bias[:, 128:256]
    ssc[pl.ds(16, 64, stride=18), :] = grad_fw[:, 0:128]
    ssc[pl.ds(16 + 64 * 18, 64, stride=18), :] = grad_fw[:, 128:256]
    ssc[pl.ds(17, 128, stride=18), :] = sm[...]
    core = own % 2
    kept[...] = ssc[pl.ds(pl.multiple_of(core * 1152, 1152), 1152), :]
    given[...] = ssc[pl.ds(pl.multiple_of((1 - core) * 1152, 1152), 1152), :].astype(BF16)


def pair_kernel(kept, taken, out):
    out[...] = (kept[...] + taken[...].astype(F32)).astype(BF16)


def mod18(x):
    return x - 18 * jnp.floor((x.astype(F32) + 0.5) / 18.0).astype(jnp.int32)


def sum_kernel(recv, out):
    pick = one_hot(mod18(iota((32, 1152), 1)) == iota((32, 1152), 0))
    total = mm(pick, recv[...]).astype(BF16)
    again = one_hot(mod18(iota((144, 32), 0)) == iota((144, 32), 1))
    block = mm(again, total).astype(BF16)
    for k in range(8):
        out[144 * k : 144 * k + 144, :] = block


def unpack_kernel(own_core, other, giw, gow, gsb, gew, geb, ghw, ghb, gfw, gsf, scr, small):
    scale = 1.0 / math.sqrt(4 * LENGTH)
    fscale = scale / 4.0
    core = own_index() % 2
    for k, recv in enumerate((own_core, other)):
        scr[k] = recv[...].astype(F32)
        first = pl.multiple_of(64 * (core if k == 0 else 1 - core), 64)
        for rb in range(2):
            for cb in range(8):
                tile = scr[k, pl.ds(8 * rb + cb, 64, stride=18), :] * scale
                rows = pl.ds(128 * rb + first, 64)
                if cb < 6:
                    giw[rows, 128 * cb : 128 * cb + 128] = tile
                else:
                    gow[rows, 128 * (cb - 6) : 128 * (cb - 6) + 128] = tile
        for n in range(2):
            small[n, pl.ds(first, 64), :] = scr[k, pl.ds(16 + n, 64, stride=18), :]
    gfw[:, 0:128] = small[0, 0:64, :] * fscale
    gfw[:, 128:256] = small[0, 64:128, :] * fscale
    second = small[1]
    ghw[...] = second[0:64, 0:64] * fscale
    gew[...] = second[64:69, 0:64] * fscale
    geb[...] = second[69:70, 0:64] * fscale
    ghb[...] = second[70:71, 0:64] * fscale
    gsf[...] = second[71:73, 0:64] * fscale
    gsb[:, 0:128] = second[73:74, :] * scale
    gsb[:, 128:256] = second[74:75, :] * scale


def call(kernel, name, out_shape, scratch=(), from_hbm=False):
    def run(*args):
        return pl.pallas_call(
            kernel,
            out_shape=out_shape,
            in_specs=[
                pl.BlockSpec(memory_space=pltpu.HBM if from_hbm else pltpu.VMEM)
                for _ in args
            ],
            scratch_shapes=list(scratch),
            compiler_params=pltpu.CompilerParams(vmem_limit_bytes=48 * 1024 * 1024),
            name=name,
        )(*args)

    return run


def exchange(x, rows, groups=None):
    count = x.shape[0] // rows
    y = x.reshape(count, rows // 2, 2, 128)
    y = lax.all_to_all(
        y, AXES, split_axis=0, concat_axis=0, axis_index_groups=groups, tiled=True
    )
    return y.reshape(count * rows, 128)


def swap_cores(x):
    return lax.ppermute(x, "batch", [(k, k ^ 1) for k in range(4)])


def sds(*shape, dtype=F32):
    return jax.ShapeDtypeStruct(shape, dtype)


def shards(
    tokens, out_grad, in_weight, out_weight, skip_bias, embed_weight, embed_bias,
    hidden_weight, hidden_bias, filter_weight, sine_freq, decay_rate,
):
    tok = tokens[0]
    og = out_grad[0]
    decay = decay_rate[None, :]
    square = sds(256, 256, dtype=BF16)
    hidden = sds(64, 64)
    inputs = (tok, og, in_weight, out_weight, embed_weight, embed_bias[None, :], hidden_weight,
              hidden_bias[None, :], filter_weight, sine_freq, decay, skip_bias[None, :])
    (slab, go, gi, v, gg, bias, emb, pre1, act1, pre2, act2,
     skip, modul, hw, fw, sf) = call(
        forward_kernel,
        "forward",
        (sds(1280, 128, dtype=BF16), square, square, square, square, sds(1, 256),
         sds(5, 64, 64), hidden, hidden, hidden, hidden, sds(1, 256),
         sds(64, 256), hidden, sds(64, 256), sds(2, 64)),
        [pltpu.VMEM(x.shape, x.dtype) for x in inputs]
        + [pltpu.VMEM((1280, 128), F32), pltpu.SemaphoreType.DMA((len(inputs),))],
        from_hbm=True,
    )(*(pltpu.with_memory_space_constraint(x, pltpu.HBM) for x in inputs))
    recv = exchange(slab, 10)
    sent = call(
        conv_kernel,
        "conv",
        sds(1280, 128, dtype=BF16),
        [
            pltpu.VMEM((1280, 128), F32),
            pltpu.VMEM((1280, 128), F32),
            pltpu.VMEM((2, 528, 256), BF16),
            pltpu.VMEM((2, 65 * 128, 128), BF16),
            pltpu.VMEM((4, 288, 128), F32),
            pltpu.VMEM((16, 256, 128), BF16),
            pltpu.VMEM((2, 520, 128), F32),
        ],
    )(recv, skip)
    recv = exchange(sent, 10)
    gtok, kept, given = call(
        backward_kernel,
        "backward",
        (square, sds(1152, 128), sds(1152, 128, dtype=BF16)),
        [
            pltpu.VMEM((1280, 128), F32),
            pltpu.VMEM((128, 256), F32),
            pltpu.VMEM((128, 128), F32),
            pltpu.VMEM((2304, 128), F32),
        ],
    )(recv, go, gi, v, gg, tok, og, in_weight, emb, pre1, act1, pre2, act2, bias, modul, hw, fw, sf)
    half = sds(1152, 128, dtype=BF16)
    slab = call(pair_kernel, "pair", half)(kept, swap_cores(given))
    by_core = [list(range(core, 128, 2)) for core in range(2)]
    recv = exchange(slab, 18, by_core)
    total = call(sum_kernel, "total", half)(recv)
    recv = exchange(total, 18, by_core)
    giw, gow, gsb, gew, geb, ghw, ghb, gfw, gsf = call(
        unpack_kernel,
        "unpack",
        (sds(256, 768), sds(256, 256), sds(1, 256), sds(5, 64), sds(1, 64), sds(64, 64),
         sds(1, 64), sds(64, 256), sds(2, 64)),
        [pltpu.VMEM((2, 1152, 128), F32), pltpu.VMEM((2, 128, 128), F32)],
    )(recv, swap_cores(recv))
    return (gtok[None], giw, gow, gsb[0], gew, geb[0], ghw, ghb[0], gfw, gsf)


def solution(mesh):
    return jax.shard_map(
        shards,
        mesh=mesh,
        in_specs=(P("batch", "seq", None),) * 2 + (P(),) * 10,
        out_specs=(P("batch", "seq", None),) + (P(),) * 9,
        check_vma=False,
    )
```

```python
import math

import jax
import jax.numpy as jnp
from jax import lax
from jax.experimental import pallas as pl
from jax.experimental.pallas import tpu as pltpu
from jax.sharding import PartitionSpec as P

F32 = jnp.float32
BF16 = jnp.bfloat16
HIGHEST = lax.Precision.HIGHEST
AXES = ("seq", "batch")
LENGTH = 8192
BANDS = 2
NN = (((1,), (0,)), ((), ()))
NT = (((1,), (1,)), ((), ()))


def mm(a, b, dims=NN):
    return lax.dot_general(a, b, dims, preferred_element_type=F32)


def mm_full(a, b, dims=NN):
    return lax.dot_general(a, b, dims, precision=HIGHEST, preferred_element_type=F32)


def iota(shape, dim):
    return lax.broadcasted_iota(jnp.int32, shape, dim)


def one_hot(cond):
    return jnp.where(cond, 1.0, 0.0).astype(BF16)


def own_index():
    return lax.axis_index("seq") * lax.axis_size("batch") + lax.axis_index("batch")


def modulation(decay, first, shape):
    pos = (first + iota(shape, 0)).astype(F32)
    return 4.0 * jnp.exp(-decay * pos) / math.sqrt(LENGTH)


def forward_kernel(
    tok_h, og_h, wi_h, wo_h, ew_h, eb_h, hw_h, hb_h, fw_h, sf_h, dr_h, sk_h,
    slab, go_o, gi_o, v_o, gg_o, bias_o, emb_o, pre1_o, act1_o, pre2_o, act2_o,
    sk_o, mod_o, hw_o, fw_o, sf_o,
    tok, og, wi, wo, ew, eb, hw, hb, fw, sf, dr, sk, scr, sems,
):
    pairs = (
        (tok_h, tok), (wi_h, wi), (og_h, og), (wo_h, wo), (sf_h, sf), (ew_h, ew), (eb_h, eb),
        (hw_h, hw), (hb_h, hb), (fw_h, fw), (dr_h, dr), (sk_h, sk),
    )
    copies = [pltpu.make_async_copy(a, b, sems.at[k]) for k, (a, b) in enumerate(pairs)]
    for c in copies:
        c.start()
    first = own_index() * 64
    scaled = (first + iota((64, 64), 0)).astype(F32) / LENGTH
    rows = [scaled]
    for band in range(1, BANDS + 1):
        angle = 2.0 * math.pi * band * scaled
        rows.append(jnp.cos(angle))
        rows.append(jnp.sin(angle))
    for c in copies:
        c.wait()
    proj = mm(tok[...], wi[...])
    go = proj[:, :256].astype(BF16)
    gi = proj[:, 256:512].astype(BF16)
    v = proj[:, 512:].astype(BF16)
    gg = mm(og[...], wo[...], NT).astype(BF16)
    go_o[...] = go
    gi_o[...] = gi
    v_o[...] = v
    gg_o[...] = gg
    mixed = (v.astype(F32) * gi.astype(F32)).astype(BF16).astype(F32)
    gc = (gg.astype(F32) * go.astype(F32)).astype(BF16).astype(F32)
    sk_o[...] = sk[...]
    hw_o[...] = hw[...]
    fw_o[...] = fw[...]
    sf_o[...] = sf[...]
    bias_o[...] = jnp.sum(gc * mixed, axis=0, keepdims=True)
    mixed_t = mixed.T
    gc_t = gc.T
    pre1 = eb[...]
    for k in range(5):
        pre1 = pre1 + rows[k] * ew[k : k + 1, :]
        emb_o[k] = rows[k]
    act1 = jnp.sin(sf[0:1, :] * pre1)
    pre2 = mm_full(act1, hw[...]) + hb[...]
    act2 = jnp.sin(sf[1:2, :] * pre2)
    pre1_o[...] = pre1
    act1_o[...] = act1
    pre2_o[...] = pre2
    act2_o[...] = act2
    modul = modulation(dr[...], first, (64, 256))
    mod_o[...] = modul
    filt = mm_full(act2, fw[...]) * modul
    side = 64 * (lax.axis_index("batch") % 2)
    place = one_hot(iota((64, 128), 1) == iota((64, 128), 0) + side)
    filt_t = mm(filt.T.astype(BF16), place)
    for ch in range(2):
        scr[pl.ds(8 + ch, 128, stride=10), :] = filt_t[128 * ch : 128 * ch + 128, :]
        for at, whole in ((0, mixed_t), (4, gc_t)):
            for half in range(2):
                scr[pl.ds(at + 2 * ch + half, 128, stride=10), :] = whole[
                    128 * ch : 128 * ch + 128, 128 * half : 128 * half + 128
                ]
    slab[...] = scr[...].astype(BF16)


def row_rolls(x, bits):
    row = iota(x.shape, 0)
    for bit in range(bits):
        x = jnp.where((row >> bit) & 1 == 1, pltpu.roll(x, 1 << bit, 1), x)
    return x


def conv_kernel(
    recv, skip, out, scr, osc, fscr, u_a, u_b, c_a, c_b, spad, spad_odd, acc, gpad, gs, gsc
):
    scr[...] = recv[...].astype(F32)
    own = own_index()
    row, col = iota((256, 256), 0), iota((256, 256), 1)
    rev256 = one_hot(row + col == 255)
    rev128 = one_hot(iota((128, 128), 0) + iota((128, 128), 1) == 127)

    def source(r):
        blk, sig = r >> 3, r & 7
        return jnp.where(sig < 4, blk * 4 + sig, 128 + (31 - blk) * 4 + sig - 4)

    perm = one_hot(source(row) == col)
    back = one_hot(source(col) == row)
    gather = [
        one_hot(iota((512, 128), 1) >> 1 == 2 * (iota((512, 128), 0) >> 4) + h) for h in range(2)
    ]
    spread_g = one_hot(iota((128, 64), 0) >> 1 == iota((128, 64), 1))
    lane, sub = iota((8, 128), 1), iota((8, 128), 0)
    lane16, sub16 = iota((16, 128), 1), iota((16, 128), 0)

    def line(r):
        return scr[pl.ds(r, 128, stride=10), :]

    mixed_up, x_revs = [], []
    for ch in range(2):
        f_in = line(8 + ch).astype(BF16)
        fscr[ch, 0:16, :] = jnp.zeros((16, 256), BF16)
        fscr[ch, 528:592, :] = jnp.zeros((64, 256), BF16)
        for h in range(2):
            fscr[ch, 16:528, 128 * h : 128 * h + 128] = row_rolls(mm(gather[h], f_in), 4).astype(BF16)
    for ch in range(2):
        xs = [line(2 * ch + h) for h in range(2)]
        gs_in = [line(4 + 2 * ch + h) for h in range(2)]
        x2 = jnp.concatenate(xs, axis=1).astype(BF16)
        g2 = jnp.concatenate(gs_in, axis=1).astype(BF16)
        g_rev = mm(g2, rev256).astype(BF16)
        up = mm(perm, jnp.concatenate([x2, g_rev], axis=0))
        mixed_up.append(up)
        spad[ch, 0:256, :] = jnp.zeros((256, 256), BF16)
        spad_odd[ch, 0:256, :] = jnp.zeros((256, 256), BF16)
        spad[ch, 256:512, :] = up.astype(BF16)
        spad_odd[ch, 256:512, :] = jnp.concatenate(
            [jnp.zeros((8, 256), F32), up[0:248, :]], axis=0
        ).astype(BF16)
        acc[ch] = jnp.zeros((256, 256), F32)
        c_b[ch, 8] = jnp.zeros((128, 128), F32)
        x_revs.append(
            jnp.concatenate([mm(rev128, x.astype(BF16), NT).astype(BF16) for x in xs], axis=1)
        )
        for h in range(2):
            at = 2 * ch + h
            gpad[at, 0:128, :] = gs_in[h]
            gpad[at, 128:288, :] = jnp.zeros((160, 128), F32)
            for s in range(4):
                gs[4 * at + s] = gpad[at, 4 * s : 4 * s + 256, :].astype(BF16)

    def build_toeplitz(q, u):
        for ch in range(2):
            for n in range(-1, 8):
                at = pl.multiple_of(64 * q + 16 * (n // 2 + 1), 16)
                this = fscr[ch, pl.ds(at, 16), 128 * (n % 2) : 128 * (n % 2) + 128]
                at = pl.multiple_of(64 * q + 16 * ((n - 1) // 2 + 1), 16)
                last = fscr[ch, pl.ds(at, 16), 128 - 128 * (n % 2) : 256 - 128 * (n % 2)]
                fresh = jnp.where(lane16 >= sub16, this, last)
                tiles = [fresh]
                for g in range(1, 8):
                    picked = jnp.where(lane16 < 128 - 16 * g, fresh, last)
                    tiles.append(pltpu.roll(picked, 16 * g, 1))
                u[ch, n + 1] = jnp.concatenate(tiles, axis=0)

    def convolve(q, u):
        at = pl.multiple_of(256 - 32 * q, 16)
        low = pl.multiple_of(240 - 32 * q, 16)
        for ch in range(2):
            left = jnp.concatenate(
                [
                    spad[ch, pl.ds(at, 256), :],
                    spad_odd[ch, pl.ds(at, 256), :],
                    spad[ch, pl.ds(low, 256), :],
                    spad_odd[ch, pl.ds(low, 256), :],
                ],
                axis=1,
            )
            right = []
            for k in range(4):
                right.append(jnp.concatenate([u[ch, 2 * k + 1], u[ch, 2 * k + 2]], axis=1))
                right.append(jnp.concatenate([u[ch, 2 * k], u[ch, 2 * k + 1]], axis=1))
            acc[ch] += mm(left, jnp.concatenate(right, axis=0))

    def correlate(q, c, c_before):
        for ch in range(2):
            c[ch, 0] = c_before[ch, 8]
            for s in range(4):
                at = pl.multiple_of(16 * q, 16)
                at_next = pl.multiple_of(16 * q + 16 * (s // 3), 16)
                g0 = gs[8 * ch + s, pl.ds(at, 128), :]
                g1 = gs[8 * ch + 4 + s, pl.ds(at, 128), :]
                g0_next = gs[8 * ch + (s + 1) % 4, pl.ds(at_next, 128), :]
                right = jnp.concatenate(
                    [
                        jnp.concatenate([g0, g1], axis=1),
                        jnp.concatenate([g1, g0_next], axis=1),
                    ],
                    axis=0,
                )
                both = mm(x_revs[ch], right)
                c[ch, 2 * s + 1] = both[:, 0:128]
                c[ch, 2 * s + 2] = both[:, 128:256]

    def diagonals(c, ch, n):
        part = None
        for g in range(16):
            old = c[ch, n, 8 * g : 8 * g + 8, :]
            new = jnp.zeros((8, 128), F32) if n == 8 else c[ch, n + 1, 8 * g : 8 * g + 8, :]
            now = pltpu.roll(jnp.where(lane + sub >= 127 - 8 * g, old, new), 8 * g + 1, 1)
            part = now if part is None else part + now
        return part

    def sum_diagonals(q, c):
        for ch in range(2):
            for n in range(8):
                to = pl.multiple_of(64 * q + 64 + 8 * n, 8)
                gsc[ch, pl.ds(to, 8), :] = diagonals(c, ch, n)

    build_toeplitz(0, u_a)

    def step(r, carry):
        q = 2 * r
        convolve(q, u_a)
        correlate(q, c_a, c_b)
        build_toeplitz(q + 1, u_b)
        sum_diagonals(q - 1, c_b)
        convolve(q + 1, u_b)
        correlate(q + 1, c_b, c_a)
        build_toeplitz(q + 2, u_a)
        sum_diagonals(q, c_a)
        return carry

    lax.fori_loop(0, 4, step, 0)
    sum_diagonals(7, c_b)

    for ch in range(2):
        mine = iota((1, 256), 1) == own + 128 * ch
        skip_now = jnp.sum(jnp.where(mine, skip[...], 0.0), axis=1, keepdims=True)
        done = (acc[ch] + skip_now * mixed_up[ch]).astype(BF16)
        apart = mm(back, done)
        conv2 = apart[0:128, :]
        gm2 = mm(apart[128:256, :].astype(BF16), rev256)
        for h in range(2):
            osc[pl.ds(2 * ch + h, 128, stride=10), :] = conv2[:, 128 * h : 128 * h + 128]
            osc[pl.ds(4 + 2 * ch + h, 128, stride=10), :] = gm2[:, 128 * h : 128 * h + 128]
        gsc[ch, 576:584, :] = diagonals(c_b, ch, 8)
        gf = row_rolls(gsc[ch, 72:584, :], 3).reshape(64, 8, 128).sum(axis=1)
        osc[pl.ds(8 + ch, 128, stride=10), :] = mm(spread_g, gf.astype(BF16))
    out[...] = osc[...].astype(BF16)


def backward_kernel(
    recv, go, gi, v, gg, tok, og, wi, emb, pre1, act1, pre2, act2, bias, modul, hw, fw, sf,
    gtok, kept, given, scr, tmp, sm, ssc,
):
    own = own_index()
    scr[...] = recv[...].astype(F32)

    def line(r):
        return scr[pl.ds(r, 128, stride=10), :]

    def whole(at):
        return jnp.concatenate(
            [
                jnp.concatenate([line(at + 2 * ch), line(at + 2 * ch + 1)], axis=1)
                for ch in range(2)
            ],
            axis=0,
        )

    conv = whole(0).T
    gm = whole(4).T
    gated_t = (go[...].astype(F32) * conv).T.astype(BF16)
    grad_ow = mm(gated_t, og[...])
    gp = jnp.concatenate(
        [
            (gg[...].astype(F32) * conv).astype(BF16),
            (gm * v[...].astype(F32)).astype(BF16),
            (gm * gi[...].astype(F32)).astype(BF16),
        ],
        axis=1,
    )
    gtok[...] = mm(gp, wi[...], NT).astype(BF16)
    grad_iw = mm(tok[...].astype(F32).T.astype(BF16), gp)
    for rb in range(2):
        for cb in range(8):
            src = grad_iw if cb < 6 else grad_ow
            at = 128 * (cb if cb < 6 else cb - 6)
            ssc[pl.ds(8 * rb + cb, 128, stride=18), :] = src[
                128 * rb : 128 * rb + 128, at : at + 128
            ]

    tmp[...] = jnp.concatenate([line(8), line(9)], axis=0).T
    gf = tmp[pl.ds(pl.multiple_of((own % 2) * 64, 64), 64), :]
    gk = gf * modul[...]
    grad_fw = mm_full(act2[...].T, gk)
    ga2 = mm_full(gk, fw[...], NT)
    cos2 = jnp.cos(sf[1:2, :] * pre2[...])
    gp2 = ga2 * sf[1:2, :] * cos2
    grad_f2 = jnp.sum(ga2 * pre2[...] * cos2, axis=0, keepdims=True)
    grad_hb = jnp.sum(gp2, axis=0, keepdims=True)
    grad_hw = mm_full(act1[...].T, gp2)
    ga1 = mm_full(gp2, hw[...], NT)
    cos1 = jnp.cos(sf[0:1, :] * pre1[...])
    gp1 = ga1 * sf[0:1, :] * cos1
    grad_f1 = jnp.sum(ga1 * pre1[...] * cos1, axis=0, keepdims=True)
    grad_eb = jnp.sum(gp1, axis=0, keepdims=True)
    sm[...] = jnp.zeros((128, 128), F32)
    sm[0:64, 0:64] = grad_hw
    for k in range(5):
        sm[64 + k : 65 + k, 0:64] = jnp.sum(emb[k] * gp1, axis=0, keepdims=True)
    sm[69:70, 0:64] = grad_eb
    sm[70:71, 0:64] = grad_hb
    sm[71:72, 0:64] = grad_f1
    sm[72:73, 0:64] = grad_f2
    sm[73:74, :] = bias[:, 0:128]
    sm[74:75, :] = bias[:, 128:256]
    ssc[pl.ds(16, 64, stride=18), :] = grad_fw[:, 0:128]
    ssc[pl.ds(16 + 64 * 18, 64, stride=18), :] = grad_fw[:, 128:256]
    ssc[pl.ds(17, 128, stride=18), :] = sm[...]
    core = own % 2
    kept[...] = ssc[pl.ds(pl.multiple_of(core * 1152, 1152), 1152), :]
    given[...] = ssc[pl.ds(pl.multiple_of((1 - core) * 1152, 1152), 1152), :].astype(BF16)


def pair_kernel(kept, taken, out):
    out[...] = (kept[...] + taken[...].astype(F32)).astype(BF16)


def mod18(x):
    return x - 18 * jnp.floor((x.astype(F32) + 0.5) / 18.0).astype(jnp.int32)


def sum_kernel(recv, out):
    pick = one_hot(mod18(iota((32, 1152), 1)) == iota((32, 1152), 0))
    total = mm(pick, recv[...]).astype(BF16)
    again = one_hot(mod18(iota((144, 32), 0)) == iota((144, 32), 1))
    block = mm(again, total).astype(BF16)
    for k in range(8):
        out[144 * k : 144 * k + 144, :] = block


def unpack_kernel(own_core, other, giw, gow, gsb, gew, geb, ghw, ghb, gfw, gsf, scr, small):
    scale = 1.0 / math.sqrt(4 * LENGTH)
    fscale = scale / 4.0
    core = own_index() % 2
    for k, recv in enumerate((own_core, other)):
        scr[k] = recv[...].astype(F32)
        first = pl.multiple_of(64 * (core if k == 0 else 1 - core), 64)
        for rb in range(2):
            for cb in range(8):
                tile = scr[k, pl.ds(8 * rb + cb, 64, stride=18), :] * scale
                rows = pl.ds(128 * rb + first, 64)
                if cb < 6:
                    giw[rows, 128 * cb : 128 * cb + 128] = tile
                else:
                    gow[rows, 128 * (cb - 6) : 128 * (cb - 6) + 128] = tile
        for n in range(2):
            small[n, pl.ds(first, 64), :] = scr[k, pl.ds(16 + n, 64, stride=18), :]
    gfw[:, 0:128] = small[0, 0:64, :] * fscale
    gfw[:, 128:256] = small[0, 64:128, :] * fscale
    second = small[1]
    ghw[...] = second[0:64, 0:64] * fscale
    gew[...] = second[64:69, 0:64] * fscale
    geb[...] = second[69:70, 0:64] * fscale
    ghb[...] = second[70:71, 0:64] * fscale
    gsf[...] = second[71:73, 0:64] * fscale
    gsb[:, 0:128] = second[73:74, :] * scale
    gsb[:, 128:256] = second[74:75, :] * scale


def call(kernel, name, out_shape, scratch=(), from_hbm=False):
    def run(*args):
        return pl.pallas_call(
            kernel,
            out_shape=out_shape,
            in_specs=[
                pl.BlockSpec(memory_space=pltpu.HBM if from_hbm else pltpu.VMEM)
                for _ in args
            ],
            scratch_shapes=list(scratch),
            compiler_params=pltpu.CompilerParams(vmem_limit_bytes=48 * 1024 * 1024),
            name=name,
        )(*args)

    return run


def exchange(x, rows, groups=None):
    count = x.shape[0] // rows
    y = x.reshape(count, rows // 2, 2, 128)
    y = lax.all_to_all(
        y, AXES, split_axis=0, concat_axis=0, axis_index_groups=groups, tiled=True
    )
    return y.reshape(count * rows, 128)


def swap_cores(x):
    return lax.ppermute(x, "batch", [(k, k ^ 1) for k in range(4)])


def sds(*shape, dtype=F32):
    return jax.ShapeDtypeStruct(shape, dtype)


def shards(
    tokens, out_grad, in_weight, out_weight, skip_bias, embed_weight, embed_bias,
    hidden_weight, hidden_bias, filter_weight, sine_freq, decay_rate,
):
    tok = tokens[0]
    og = out_grad[0]
    decay = decay_rate[None, :]
    square = sds(256, 256, dtype=BF16)
    hidden = sds(64, 64)
    inputs = (tok, og, in_weight, out_weight, embed_weight, embed_bias[None, :], hidden_weight,
              hidden_bias[None, :], filter_weight, sine_freq, decay, skip_bias[None, :])
    (slab, go, gi, v, gg, bias, emb, pre1, act1, pre2, act2,
     skip, modul, hw, fw, sf) = call(
        forward_kernel,
        "forward",
        (sds(1280, 128, dtype=BF16), square, square, square, square, sds(1, 256),
         sds(5, 64, 64), hidden, hidden, hidden, hidden, sds(1, 256),
         sds(64, 256), hidden, sds(64, 256), sds(2, 64)),
        [pltpu.VMEM(x.shape, x.dtype) for x in inputs]
        + [pltpu.VMEM((1280, 128), F32), pltpu.SemaphoreType.DMA((len(inputs),))],
        from_hbm=True,
    )(*(pltpu.with_memory_space_constraint(x, pltpu.HBM) for x in inputs))
    recv = exchange(slab, 10)
    sent = call(
        conv_kernel,
        "conv",
        sds(1280, 128, dtype=BF16),
        [
            pltpu.VMEM((1280, 128), F32),
            pltpu.VMEM((1280, 128), F32),
            pltpu.VMEM((2, 592, 256), BF16),
            pltpu.VMEM((2, 9, 128, 128), BF16),
            pltpu.VMEM((2, 9, 128, 128), BF16),
            pltpu.VMEM((2, 9, 128, 128), F32),
            pltpu.VMEM((2, 9, 128, 128), F32),
            pltpu.VMEM((2, 512, 256), BF16),
            pltpu.VMEM((2, 512, 256), BF16),
            pltpu.VMEM((2, 256, 256), F32),
            pltpu.VMEM((4, 288, 128), F32),
            pltpu.VMEM((16, 256, 128), BF16),
            pltpu.VMEM((2, 584, 128), F32),
        ],
    )(recv, skip)
    recv = exchange(sent, 10)
    gtok, kept, given = call(
        backward_kernel,
        "backward",
        (square, sds(1152, 128), sds(1152, 128, dtype=BF16)),
        [
            pltpu.VMEM((1280, 128), F32),
            pltpu.VMEM((128, 256), F32),
            pltpu.VMEM((128, 128), F32),
            pltpu.VMEM((2304, 128), F32),
        ],
    )(recv, go, gi, v, gg, tok, og, in_weight, emb, pre1, act1, pre2, act2, bias, modul, hw, fw, sf)
    half = sds(1152, 128, dtype=BF16)
    slab = call(pair_kernel, "pair", half)(kept, swap_cores(given))
    by_core = [list(range(core, 128, 2)) for core in range(2)]
    recv = exchange(slab, 18, by_core)
    total = call(sum_kernel, "total", half)(recv)
    recv = exchange(total, 18, by_core)
    giw, gow, gsb, gew, geb, ghw, ghb, gfw, gsf = call(
        unpack_kernel,
        "unpack",
        (sds(256, 768), sds(256, 256), sds(1, 256), sds(5, 64), sds(1, 64), sds(64, 64),
         sds(1, 64), sds(64, 256), sds(2, 64)),
        [pltpu.VMEM((2, 1152, 128), F32), pltpu.VMEM((2, 128, 128), F32)],
    )(recv, swap_cores(recv))
    return (gtok[None], giw, gow, gsb[0], gew, geb[0], ghw, ghb[0], gfw, gsf)


def solution(mesh):
    return jax.shard_map(
        shards,
        mesh=mesh,
        in_specs=(P("batch", "seq", None),) * 2 + (P(),) * 10,
        out_specs=(P("batch", "seq", None),) + (P(),) * 9,
        check_vma=False,
    )
```

```python
import math

import jax
import jax.numpy as jnp
from jax import lax
from jax.experimental import pallas as pl
from jax.experimental.pallas import tpu as pltpu
from jax.sharding import PartitionSpec as P

F32 = jnp.float32
BF16 = jnp.bfloat16
HIGHEST = lax.Precision.HIGHEST
AXES = ("seq", "batch")
LENGTH = 8192
BANDS = 2
NN = (((1,), (0,)), ((), ()))
NT = (((1,), (1,)), ((), ()))


def mm(a, b, dims=NN):
    return lax.dot_general(a, b, dims, preferred_element_type=F32)


def mm_full(a, b, dims=NN):
    return lax.dot_general(a, b, dims, precision=HIGHEST, preferred_element_type=F32)


def iota(shape, dim):
    return lax.broadcasted_iota(jnp.int32, shape, dim)


def one_hot(cond):
    return jnp.where(cond, 1.0, 0.0).astype(BF16)


def own_index():
    return lax.axis_index("seq") * lax.axis_size("batch") + lax.axis_index("batch")


def modulation(decay, first, shape):
    pos = (first + iota(shape, 0)).astype(F32)
    return 4.0 * jnp.exp(-decay * pos) / math.sqrt(LENGTH)


def forward_kernel(
    tok_h, og_h, wi_h, wo_h, ew_h, eb_h, hw_h, hb_h, fw_h, sf_h, dr_h, sk_h,
    slab, go_o, gi_o, v_o, gg_o, bias_o, emb_o, pre1_o, act1_o, pre2_o, act2_o,
    sk_o, mod_o, hw_o, fw_o, sf_o,
    tok, og, wi, wo, ew, eb, hw, hb, fw, sf, dr, sk, scr, sems,
):
    pairs = (
        (tok_h, tok), (wi_h, wi), (og_h, og), (wo_h, wo), (sf_h, sf), (ew_h, ew), (eb_h, eb),
        (hw_h, hw), (hb_h, hb), (fw_h, fw), (dr_h, dr), (sk_h, sk),
    )
    copies = [pltpu.make_async_copy(a, b, sems.at[k]) for k, (a, b) in enumerate(pairs)]
    for c in copies:
        c.start()
    first = own_index() * 64
    scaled = (first + iota((64, 64), 0)).astype(F32) / LENGTH
    rows = [scaled]
    for band in range(1, BANDS + 1):
        angle = 2.0 * math.pi * band * scaled
        rows.append(jnp.cos(angle))
        rows.append(jnp.sin(angle))
    for c in copies:
        c.wait()
    proj = mm(tok[...], wi[...])
    go = proj[:, :256].astype(BF16)
    gi = proj[:, 256:512].astype(BF16)
    v = proj[:, 512:].astype(BF16)
    gg = mm(og[...], wo[...], NT).astype(BF16)
    go_o[...] = go
    gi_o[...] = gi
    v_o[...] = v
    gg_o[...] = gg
    mixed = (v.astype(F32) * gi.astype(F32)).astype(BF16).astype(F32)
    gc = (gg.astype(F32) * go.astype(F32)).astype(BF16).astype(F32)
    sk_o[...] = sk[...]
    hw_o[...] = hw[...]
    fw_o[...] = fw[...]
    sf_o[...] = sf[...]
    bias_o[...] = jnp.sum(gc * mixed, axis=0, keepdims=True)
    mixed_t = mixed.T
    gc_t = gc.T
    pre1 = eb[...]
    for k in range(5):
        pre1 = pre1 + rows[k] * ew[k : k + 1, :]
        emb_o[k] = rows[k]
    act1 = jnp.sin(sf[0:1, :] * pre1)
    pre2 = mm_full(act1, hw[...]) + hb[...]
    act2 = jnp.sin(sf[1:2, :] * pre2)
    pre1_o[...] = pre1
    act1_o[...] = act1
    pre2_o[...] = pre2
    act2_o[...] = act2
    modul = modulation(dr[...], first, (64, 256))
    mod_o[...] = modul
    filt = mm_full(act2, fw[...]) * modul
    side = 64 * (lax.axis_index("batch") % 2)
    place = one_hot(iota((64, 128), 1) == iota((64, 128), 0) + side)
    filt_t = mm(filt.T.astype(BF16), place)
    for ch in range(2):
        scr[pl.ds(8 + ch, 128, stride=10), :] = filt_t[128 * ch : 128 * ch + 128, :]
        for at, whole in ((0, mixed_t), (4, gc_t)):
            for half in range(2):
                scr[pl.ds(at + 2 * ch + half, 128, stride=10), :] = whole[
                    128 * ch : 128 * ch + 128, 128 * half : 128 * half + 128
                ]
    slab[...] = scr[...].astype(BF16)


def row_rolls(x, bits):
    row = iota(x.shape, 0)
    for bit in range(bits):
        x = jnp.where((row >> bit) & 1 == 1, pltpu.roll(x, 1 << bit, 1), x)
    return x


def conv_kernel(
    recv, skip, out, scr, osc, fscr, u_a, u_b, c_a, c_b, spad, spad_odd, acc, gpad, gs, gsc
):
    scr[...] = recv[...].astype(F32)
    own = own_index()
    row, col = iota((256, 256), 0), iota((256, 256), 1)
    rev256 = one_hot(row + col == 255)
    rev128 = one_hot(iota((128, 128), 0) + iota((128, 128), 1) == 127)

    def source(r):
        blk, sig = r >> 3, r & 7
        return jnp.where(sig < 4, blk * 4 + sig, 128 + (31 - blk) * 4 + sig - 4)

    perm = one_hot(source(row) == col)
    weave = one_hot(((row >> 2) & 1) * 128 + (row >> 3) * 4 + (row & 3) == col)
    back = one_hot(source(col) == row)
    gather = [
        one_hot(iota((512, 128), 1) >> 1 == 2 * (iota((512, 128), 0) >> 4) + h) for h in range(2)
    ]
    spread_g = one_hot(iota((128, 64), 0) >> 1 == iota((128, 64), 1))
    lane, sub = iota((8, 128), 1), iota((8, 128), 0)
    lane16, sub16 = iota((16, 128), 1), iota((16, 128), 0)

    def line(r):
        return scr[pl.ds(r, 128, stride=10), :]

    mixed_up, x_revs = [], []
    for ch in range(2):
        f_in = line(8 + ch).astype(BF16)
        fscr[ch, 0:16, :] = jnp.zeros((16, 256), BF16)
        fscr[ch, 528:592, :] = jnp.zeros((64, 256), BF16)
        for h in range(2):
            fscr[ch, 16:528, 128 * h : 128 * h + 128] = row_rolls(mm(gather[h], f_in), 4).astype(BF16)
    for ch in range(2):
        xs = [line(2 * ch + h) for h in range(2)]
        gs_in = [line(4 + 2 * ch + h) for h in range(2)]
        x2 = jnp.concatenate(xs, axis=1).astype(BF16)
        g2 = jnp.concatenate(gs_in, axis=1).astype(BF16)
        g_rev = mm(g2, rev256).astype(BF16)
        up = mm(perm, jnp.concatenate([x2, g_rev], axis=0))
        mixed_up.append(up)
        spad[ch, 0:256, :] = jnp.zeros((256, 256), BF16)
        spad_odd[ch, 0:256, :] = jnp.zeros((256, 256), BF16)
        spad[ch, 256:512, :] = up.astype(BF16)
        spad_odd[ch, 256:512, :] = jnp.concatenate(
            [jnp.zeros((8, 256), F32), up[0:248, :]], axis=0
        ).astype(BF16)
        acc[ch] = jnp.zeros((256, 256), F32)
        c_b[ch, 8] = jnp.zeros((128, 128), F32)
        woven = mm(
            weave,
            jnp.concatenate(
                [jnp.concatenate([xs[h], gs_in[h]], axis=1) for h in range(2)], axis=0
            ).astype(BF16),
        )
        x_revs.append(mm(rev128, woven[:, 0:128].astype(BF16), NT).astype(BF16))
        gpad[ch, 0:256, :] = woven[:, 128:256]
        gpad[ch, 256:272, :] = jnp.zeros((16, 128), F32)
        for s in range(4):
            gs[4 * ch + s, 0:256, :] = gpad[ch, 4 * s : 4 * s + 256, :].astype(BF16)
            gs[4 * ch + s, 256:384, :] = jnp.zeros((128, 128), BF16)

    def build_toeplitz(q, u):
        for ch in range(2):
            for n in range(-1, 8):
                at = pl.multiple_of(64 * q + 16 * (n // 2 + 1), 16)
                this = fscr[ch, pl.ds(at, 16), 128 * (n % 2) : 128 * (n % 2) + 128]
                at = pl.multiple_of(64 * q + 16 * ((n - 1) // 2 + 1), 16)
                last = fscr[ch, pl.ds(at, 16), 128 - 128 * (n % 2) : 256 - 128 * (n % 2)]
                fresh = jnp.where(lane16 >= sub16, this, last)
                tiles = [fresh]
                for g in range(1, 8):
                    picked = jnp.where(lane16 < 128 - 16 * g, fresh, last)
                    tiles.append(pltpu.roll(picked, 16 * g, 1))
                u[ch, n + 1] = jnp.concatenate(tiles, axis=0)

    def convolve(q, u, late):
        skipped = 128 if late else 0
        at = pl.multiple_of(256 - 32 * q + skipped, 16)
        low = pl.multiple_of(240 - 32 * q + skipped, 16)
        count = 256 - skipped
        for ch in range(2):
            left = jnp.concatenate(
                [
                    spad[ch, pl.ds(at, count), :],
                    spad_odd[ch, pl.ds(at, count), :],
                    spad[ch, pl.ds(low, count), :],
                    spad_odd[ch, pl.ds(low, count), :],
                ],
                axis=1,
            )
            right = []
            for k in range(4):
                right.append(jnp.concatenate([u[ch, 2 * k + 1], u[ch, 2 * k + 2]], axis=1))
                right.append(jnp.concatenate([u[ch, 2 * k], u[ch, 2 * k + 1]], axis=1))
            acc[ch, skipped:256, :] += mm(left, jnp.concatenate(right, axis=0))

    def correlate(q, c, c_before, late):
        count = 128 if late else 256
        for ch in range(2):
            c[ch, 0] = c_before[ch, 8]
            for s in range(4):
                at = pl.multiple_of(32 * q + 16 * (s // 2), 16)
                right = jnp.concatenate(
                    [gs[4 * ch + (2 * s + odd) % 4, pl.ds(at, count), :] for odd in range(2)],
                    axis=1,
                )
                both = mm(x_revs[ch][:, 0:count], right)
                c[ch, 2 * s + 1] = both[:, 0:128]
                c[ch, 2 * s + 2] = both[:, 128:256]

    def diagonals(c, ch, n):
        part = None
        for g in range(16):
            old = c[ch, n, 8 * g : 8 * g + 8, :]
            new = jnp.zeros((8, 128), F32) if n == 8 else c[ch, n + 1, 8 * g : 8 * g + 8, :]
            now = pltpu.roll(jnp.where(lane + sub >= 127 - 8 * g, old, new), 8 * g + 1, 1)
            part = now if part is None else part + now
        return part

    def sum_diagonals(q, c):
        for ch in range(2):
            for n in range(8):
                to = pl.multiple_of(64 * q + 64 + 8 * n, 8)
                gsc[ch, pl.ds(to, 8), :] = diagonals(c, ch, n)

    build_toeplitz(0, u_a)

    def step(r, late):
        q = 2 * r
        convolve(q, u_a, late)
        correlate(q, c_a, c_b, late)
        build_toeplitz(q + 1, u_b)
        if r > 0:
            sum_diagonals(q - 1, c_b)
        convolve(q + 1, u_b, late)
        correlate(q + 1, c_b, c_a, late)
        if r < 3:
            build_toeplitz(q + 2, u_a)
        sum_diagonals(q, c_a)

    def run_step(late):
        def run(r, carry):
            step(r, late)
            return carry

        return run

    for r in range(4):
        step(r, r >= 2)
    sum_diagonals(7, c_b)

    for ch in range(2):
        mine = iota((1, 256), 1) == own + 128 * ch
        skip_now = jnp.sum(jnp.where(mine, skip[...], 0.0), axis=1, keepdims=True)
        done = (acc[ch] + skip_now * mixed_up[ch]).astype(BF16)
        apart = mm(back, done)
        conv2 = apart[0:128, :]
        gm2 = mm(apart[128:256, :].astype(BF16), rev256)
        for h in range(2):
            osc[pl.ds(2 * ch + h, 128, stride=10), :] = conv2[:, 128 * h : 128 * h + 128]
            osc[pl.ds(4 + 2 * ch + h, 128, stride=10), :] = gm2[:, 128 * h : 128 * h + 128]
        gsc[ch, 576:584, :] = diagonals(c_b, ch, 8)
        gf = row_rolls(gsc[ch, 72:584, :], 3).reshape(64, 8, 128).sum(axis=1)
        osc[pl.ds(8 + ch, 128, stride=10), :] = mm(spread_g, gf.astype(BF16))
    out[...] = osc[...].astype(BF16)


def backward_kernel(
    recv, go, gi, v, gg, tok, og, emb, pre1, act1, pre2, act2, bias, modul, hw, fw, sf,
    gp_o, kept, given, scr, tmp, sm, ssc,
):
    own = own_index()
    scr[...] = recv[...].astype(F32)

    def line(r):
        return scr[pl.ds(r, 128, stride=10), :]

    def whole(at):
        return jnp.concatenate(
            [
                jnp.concatenate([line(at + 2 * ch), line(at + 2 * ch + 1)], axis=1)
                for ch in range(2)
            ],
            axis=0,
        )

    conv = whole(0).T
    gm = whole(4).T
    gated_t = (go[...].astype(F32) * conv).T.astype(BF16)
    grad_ow = mm(gated_t, og[...])
    gp = jnp.concatenate(
        [
            (gg[...].astype(F32) * conv).astype(BF16),
            (gm * v[...].astype(F32)).astype(BF16),
            (gm * gi[...].astype(F32)).astype(BF16),
        ],
        axis=1,
    )
    gp_o[...] = gp
    grad_iw = mm(tok[...].astype(F32).T.astype(BF16), gp)
    for rb in range(2):
        for cb in range(8):
            src = grad_iw if cb < 6 else grad_ow
            at = 128 * (cb if cb < 6 else cb - 6)
            ssc[pl.ds(8 * rb + cb, 128, stride=18), :] = src[
                128 * rb : 128 * rb + 128, at : at + 128
            ]

    tmp[...] = jnp.concatenate([line(8), line(9)], axis=0).T
    gf = tmp[pl.ds(pl.multiple_of((own % 2) * 64, 64), 64), :]
    gk = gf * modul[...]
    grad_fw = mm_full(act2[...].T, gk)
    ga2 = mm_full(gk, fw[...], NT)
    cos2 = jnp.cos(sf[1:2, :] * pre2[...])
    gp2 = ga2 * sf[1:2, :] * cos2
    grad_f2 = jnp.sum(ga2 * pre2[...] * cos2, axis=0, keepdims=True)
    grad_hb = jnp.sum(gp2, axis=0, keepdims=True)
    grad_hw = mm_full(act1[...].T, gp2)
    ga1 = mm_full(gp2, hw[...], NT)
    cos1 = jnp.cos(sf[0:1, :] * pre1[...])
    gp1 = ga1 * sf[0:1, :] * cos1
    grad_f1 = jnp.sum(ga1 * pre1[...] * cos1, axis=0, keepdims=True)
    grad_eb = jnp.sum(gp1, axis=0, keepdims=True)
    sm[...] = jnp.zeros((128, 128), F32)
    sm[0:64, 0:64] = grad_hw
    for k in range(5):
        sm[64 + k : 65 + k, 0:64] = jnp.sum(emb[k] * gp1, axis=0, keepdims=True)
    sm[69:70, 0:64] = grad_eb
    sm[70:71, 0:64] = grad_hb
    sm[71:72, 0:64] = grad_f1
    sm[72:73, 0:64] = grad_f2
    sm[73:74, :] = bias[:, 0:128]
    sm[74:75, :] = bias[:, 128:256]
    ssc[pl.ds(16, 64, stride=18), :] = grad_fw[:, 0:128]
    ssc[pl.ds(16 + 64 * 18, 64, stride=18), :] = grad_fw[:, 128:256]
    ssc[pl.ds(17, 128, stride=18), :] = sm[...]
    core = own % 2
    kept[...] = ssc[pl.ds(pl.multiple_of(core * 1152, 1152), 1152), :]
    given[...] = ssc[pl.ds(pl.multiple_of((1 - core) * 1152, 1152), 1152), :].astype(BF16)


def token_kernel(gp, wi, gtok):
    gtok[...] = mm(gp[...], wi[...], NT).astype(BF16)


def pair_kernel(kept, taken, out):
    out[...] = (kept[...] + taken[...].astype(F32)).astype(BF16)


def mod18(x):
    return x - 18 * jnp.floor((x.astype(F32) + 0.5) / 18.0).astype(jnp.int32)


def sum_kernel(recv, out):
    pick = one_hot(mod18(iota((32, 1152), 1)) == iota((32, 1152), 0))
    total = mm(pick, recv[...]).astype(BF16)
    again = one_hot(mod18(iota((144, 32), 0)) == iota((144, 32), 1))
    block = mm(again, total).astype(BF16)
    for k in range(8):
        out[144 * k : 144 * k + 144, :] = block


def unpack_kernel(own_core, other, giw, gow, gsb, gew, geb, ghw, ghb, gfw, gsf, scr, small):
    scale = 1.0 / math.sqrt(4 * LENGTH)
    fscale = scale / 4.0
    core = own_index() % 2
    for k, recv in enumerate((own_core, other)):
        scr[k] = recv[...].astype(F32)
        first = pl.multiple_of(64 * (core if k == 0 else 1 - core), 64)
        for rb in range(2):
            for cb in range(8):
                tile = scr[k, pl.ds(8 * rb + cb, 64, stride=18), :] * scale
                rows = pl.ds(128 * rb + first, 64)
                if cb < 6:
                    giw[rows, 128 * cb : 128 * cb + 128] = tile
                else:
                    gow[rows, 128 * (cb - 6) : 128 * (cb - 6) + 128] = tile
        for n in range(2):
            small[n, pl.ds(first, 64), :] = scr[k, pl.ds(16 + n, 64, stride=18), :]
    gfw[:, 0:128] = small[0, 0:64, :] * fscale
    gfw[:, 128:256] = small[0, 64:128, :] * fscale
    second = small[1]
    ghw[...] = second[0:64, 0:64] * fscale
    gew[...] = second[64:69, 0:64] * fscale
    geb[...] = second[69:70, 0:64] * fscale
    ghb[...] = second[70:71, 0:64] * fscale
    gsf[...] = second[71:73, 0:64] * fscale
    gsb[:, 0:128] = second[73:74, :] * scale
    gsb[:, 128:256] = second[74:75, :] * scale


def call(kernel, name, out_shape, scratch=(), from_hbm=False):
    def run(*args):
        return pl.pallas_call(
            kernel,
            out_shape=out_shape,
            in_specs=[
                pl.BlockSpec(memory_space=pltpu.HBM if from_hbm else pltpu.VMEM) for _ in args
            ],
            scratch_shapes=list(scratch),
            compiler_params=pltpu.CompilerParams(vmem_limit_bytes=48 * 1024 * 1024),
            name=name,
        )(*args)

    return run


def conv_scratch():
    return [
        pltpu.VMEM((1280, 128), F32),
        pltpu.VMEM((1280, 128), F32),
        pltpu.VMEM((2, 592, 256), BF16),
        pltpu.VMEM((2, 9, 128, 128), BF16),
        pltpu.VMEM((2, 9, 128, 128), BF16),
        pltpu.VMEM((2, 9, 128, 128), F32),
        pltpu.VMEM((2, 9, 128, 128), F32),
        pltpu.VMEM((2, 512, 256), BF16),
        pltpu.VMEM((2, 512, 256), BF16),
        pltpu.VMEM((2, 256, 256), F32),
        pltpu.VMEM((2, 272, 128), F32),
        pltpu.VMEM((8, 384, 128), BF16),
        pltpu.VMEM((2, 584, 128), F32),
    ]


def exchange(x, rows, groups=None):
    count = x.shape[0] // rows
    y = x.reshape(count, rows // 2, 2, 128)
    y = lax.all_to_all(
        y, AXES, split_axis=0, concat_axis=0, axis_index_groups=groups, tiled=True
    )
    return y.reshape(count * rows, 128)


def swap_cores(x):
    return lax.ppermute(x, "batch", [(k, k ^ 1) for k in range(4)])


def sds(*shape, dtype=F32):
    return jax.ShapeDtypeStruct(shape, dtype)


def shards(
    tokens, out_grad, in_weight, out_weight, skip_bias, embed_weight, embed_bias,
    hidden_weight, hidden_bias, filter_weight, sine_freq, decay_rate,
):
    tok = tokens[0]
    og = out_grad[0]
    decay = decay_rate[None, :]
    square = sds(256, 256, dtype=BF16)
    hidden = sds(64, 64)
    inputs = (tok, og, in_weight, out_weight, embed_weight, embed_bias[None, :], hidden_weight,
              hidden_bias[None, :], filter_weight, sine_freq, decay, skip_bias[None, :])
    (slab, go, gi, v, gg, bias, emb, pre1, act1, pre2, act2,
     skip, modul, hw, fw, sf) = call(
        forward_kernel,
        "forward",
        (sds(1280, 128, dtype=BF16), square, square, square, square, sds(1, 256),
         sds(5, 64, 64), hidden, hidden, hidden, hidden, sds(1, 256),
         sds(64, 256), hidden, sds(64, 256), sds(2, 64)),
        [pltpu.VMEM(x.shape, x.dtype) for x in inputs]
        + [pltpu.VMEM((1280, 128), F32), pltpu.SemaphoreType.DMA((len(inputs),))],
        from_hbm=True,
    )(*(pltpu.with_memory_space_constraint(x, pltpu.HBM) for x in inputs))
    recv = exchange(slab, 10)
    sent = call(
        conv_kernel,
        "conv",
        sds(1280, 128, dtype=BF16),
        conv_scratch(),
    )(recv, skip)
    recv = exchange(sent, 10)
    gp, kept, given = call(
        backward_kernel,
        "backward",
        (sds(256, 768, dtype=BF16), sds(1152, 128), sds(1152, 128, dtype=BF16)),
        [
            pltpu.VMEM((1280, 128), F32),
            pltpu.VMEM((128, 256), F32),
            pltpu.VMEM((128, 128), F32),
            pltpu.VMEM((2304, 128), F32),
        ],
    )(recv, go, gi, v, gg, tok, og, emb, pre1, act1, pre2, act2, bias, modul, hw, fw, sf)
    gtok = call(token_kernel, "tokens", square)(gp, in_weight)
    half = sds(1152, 128, dtype=BF16)
    slab = call(pair_kernel, "pair", half)(kept, swap_cores(given))
    by_core = [list(range(core, 128, 2)) for core in range(2)]
    recv = exchange(slab, 18, by_core)
    total = call(sum_kernel, "total", half)(recv)
    recv = exchange(total, 18, by_core)
    giw, gow, gsb, gew, geb, ghw, ghb, gfw, gsf = call(
        unpack_kernel,
        "unpack",
        (sds(256, 768), sds(256, 256), sds(1, 256), sds(5, 64), sds(1, 64), sds(64, 64),
         sds(1, 64), sds(64, 256), sds(2, 64)),
        [pltpu.VMEM((2, 1152, 128), F32), pltpu.VMEM((2, 128, 128), F32)],
    )(recv, swap_cores(recv))
    return (gtok[None], giw, gow, gsb[0], gew, geb[0], ghw, ghb[0], gfw, gsf)


def solution(mesh):
    return jax.shard_map(
        shards,
        mesh=mesh,
        in_specs=(P("batch", "seq", None),) * 2 + (P(),) * 10,
        out_specs=(P("batch", "seq", None),) + (P(),) * 9,
        check_vma=False,
    )
```

```python
import math

import jax
import jax.numpy as jnp
from jax import lax
from jax.experimental import pallas as pl
from jax.experimental.pallas import tpu as pltpu
from jax.sharding import PartitionSpec as P

F32 = jnp.float32
BF16 = jnp.bfloat16
HIGHEST = lax.Precision.HIGHEST
AXES = ("seq", "batch")
LENGTH = 8192
BANDS = 2
NN = (((1,), (0,)), ((), ()))
NT = (((1,), (1,)), ((), ()))


def mm(a, b, dims=NN):
    return lax.dot_general(a, b, dims, preferred_element_type=F32)


def mm_full(a, b, dims=NN):
    return lax.dot_general(a, b, dims, precision=HIGHEST, preferred_element_type=F32)


def iota(shape, dim):
    return lax.broadcasted_iota(jnp.int32, shape, dim)


def one_hot(cond):
    return jnp.where(cond, 1.0, 0.0).astype(BF16)


def own_index():
    return lax.axis_index("seq") * lax.axis_size("batch") + lax.axis_index("batch")


def modulation(decay, first, shape):
    pos = (first + iota(shape, 0)).astype(F32)
    return 4.0 * jnp.exp(-decay * pos) / math.sqrt(LENGTH)


def forward_kernel(
    tok_h, og_h, wi_h, wo_h, ew_h, eb_h, hw_h, hb_h, fw_h, sf_h, dr_h, sk_h,
    slab, go_o, gi_o, v_o, gg_o, bias_o, emb_o, pre1_o, act1_o, pre2_o, act2_o,
    sk_o, mod_o, hw_o, fw_o, sf_o,
    tok, og, wi, wo, ew, eb, hw, hb, fw, sf, dr, sk, scr, sems,
):
    pairs = (
        (tok_h, tok), (wi_h, wi), (og_h, og), (wo_h, wo), (sf_h, sf), (ew_h, ew), (eb_h, eb),
        (hw_h, hw), (hb_h, hb), (fw_h, fw), (dr_h, dr), (sk_h, sk),
    )
    copies = [pltpu.make_async_copy(a, b, sems.at[k]) for k, (a, b) in enumerate(pairs)]
    for c in copies:
        c.start()
    first = own_index() * 64
    scaled = (first + iota((64, 64), 0)).astype(F32) / LENGTH
    rows = [scaled]
    for band in range(1, BANDS + 1):
        angle = 2.0 * math.pi * band * scaled
        rows.append(jnp.cos(angle))
        rows.append(jnp.sin(angle))
    for c in copies:
        c.wait()
    proj = mm(tok[...], wi[...])
    go = proj[:, :256].astype(BF16)
    gi = proj[:, 256:512].astype(BF16)
    v = proj[:, 512:].astype(BF16)
    gg = mm(og[...], wo[...], NT).astype(BF16)
    go_o[...] = go
    gi_o[...] = gi
    v_o[...] = v
    gg_o[...] = gg
    mixed = (v.astype(F32) * gi.astype(F32)).astype(BF16).astype(F32)
    gc = (gg.astype(F32) * go.astype(F32)).astype(BF16).astype(F32)
    sk_o[...] = sk[...]
    hw_o[...] = hw[...]
    fw_o[...] = fw[...]
    sf_o[...] = sf[...]
    bias_o[...] = jnp.sum(gc * mixed, axis=0, keepdims=True)
    mixed_t = mixed.T
    gc_t = gc.T
    pre1 = eb[...]
    for k in range(5):
        pre1 = pre1 + rows[k] * ew[k : k + 1, :]
        emb_o[k] = rows[k]
    act1 = jnp.sin(sf[0:1, :] * pre1)
    pre2 = mm_full(act1, hw[...]) + hb[...]
    act2 = jnp.sin(sf[1:2, :] * pre2)
    pre1_o[...] = pre1
    act1_o[...] = act1
    pre2_o[...] = pre2
    act2_o[...] = act2
    modul = modulation(dr[...], first, (64, 256))
    mod_o[...] = modul
    filt = mm_full(act2, fw[...]) * modul
    side = 64 * (lax.axis_index("batch") % 2)
    place = one_hot(iota((64, 128), 1) == iota((64, 128), 0) + side)
    filt_t = mm(filt.T.astype(BF16), place)
    for ch in range(2):
        scr[pl.ds(8 + ch, 128, stride=10), :] = filt_t[128 * ch : 128 * ch + 128, :]
        for at, whole in ((0, mixed_t), (4, gc_t)):
            for half in range(2):
                scr[pl.ds(at + 2 * ch + half, 128, stride=10), :] = whole[
                    128 * ch : 128 * ch + 128, 128 * half : 128 * half + 128
                ]
    slab[...] = scr[0:1280, :].astype(BF16)


def row_rolls(x, bits):
    row = iota(x.shape, 0)
    for bit in range(bits):
        x = jnp.where((row >> bit) & 1 == 1, pltpu.roll(x, 1 << bit, 1), x)
    return x


def conv_kernel(
    recv, skip, out, scr, osc, fscr, u_a, u_b, c_a, c_b, spad, spad_odd, acc, gpad, gs, gsc
):
    scr[0:1280, :] = recv[...].astype(F32)
    own = own_index()
    row, col = iota((256, 256), 0), iota((256, 256), 1)
    rev256 = one_hot(row + col == 255)
    rev128 = one_hot(iota((128, 128), 0) + iota((128, 128), 1) == 127)

    def source(r):
        blk, sig = r >> 3, r & 7
        return jnp.where(sig < 4, blk * 4 + sig, 128 + (31 - blk) * 4 + sig - 4)

    perm = one_hot(source(row) == col)
    weave = one_hot(((row >> 2) & 1) * 128 + (row >> 3) * 4 + (row & 3) == col)
    back = one_hot(source(col) == row)
    gather = [
        one_hot(iota((512, 128), 1) >> 1 == 2 * (iota((512, 128), 0) >> 4) + h) for h in range(2)
    ]
    spread_g = one_hot(iota((128, 64), 0) >> 1 == iota((128, 64), 1))
    lane, sub = iota((8, 128), 1), iota((8, 128), 0)
    lane16, sub16 = iota((16, 128), 1), iota((16, 128), 0)

    def line(r):
        return scr[pl.ds(r, 128, stride=10), :]

    mixed_up, x_revs = [], []
    for ch in range(2):
        f_in = line(8 + ch).astype(BF16)
        fscr[ch, 0:16, :] = jnp.zeros((16, 256), BF16)
        fscr[ch, 528:592, :] = jnp.zeros((64, 256), BF16)
        for h in range(2):
            fscr[ch, 16:528, 128 * h : 128 * h + 128] = row_rolls(mm(gather[h], f_in), 4).astype(BF16)
    for ch in range(2):
        xs = [line(2 * ch + h) for h in range(2)]
        gs_in = [line(4 + 2 * ch + h) for h in range(2)]
        x2 = jnp.concatenate(xs, axis=1).astype(BF16)
        g2 = jnp.concatenate(gs_in, axis=1).astype(BF16)
        g_rev = mm(g2, rev256).astype(BF16)
        up = mm(perm, jnp.concatenate([x2, g_rev], axis=0))
        mixed_up.append(up)
        spad[ch, 0:256, :] = jnp.zeros((256, 256), BF16)
        spad_odd[ch, 0:256, :] = jnp.zeros((256, 256), BF16)
        spad[ch, 256:512, :] = up.astype(BF16)
        spad_odd[ch, 256:512, :] = jnp.concatenate(
            [jnp.zeros((8, 256), F32), up[0:248, :]], axis=0
        ).astype(BF16)
        acc[ch] = jnp.zeros((256, 256), F32)
        c_b[ch, 8] = jnp.zeros((128, 128), F32)
        woven = mm(
            weave,
            jnp.concatenate(
                [jnp.concatenate([xs[h], gs_in[h]], axis=1) for h in range(2)], axis=0
            ).astype(BF16),
        )
        x_revs.append(mm(rev128, woven[:, 0:128].astype(BF16), NT).astype(BF16))
        gpad[ch, 0:256, :] = woven[:, 128:256]
        gpad[ch, 256:272, :] = jnp.zeros((16, 128), F32)
        for s in range(4):
            gs[4 * ch + s, 0:256, :] = gpad[ch, 4 * s : 4 * s + 256, :].astype(BF16)
            gs[4 * ch + s, 256:384, :] = jnp.zeros((128, 128), BF16)

    def build_toeplitz(q, u):
        for ch in range(2):
            for n in range(-1, 8):
                at = pl.multiple_of(64 * q + 16 * (n // 2 + 1), 16)
                this = fscr[ch, pl.ds(at, 16), 128 * (n % 2) : 128 * (n % 2) + 128]
                at = pl.multiple_of(64 * q + 16 * ((n - 1) // 2 + 1), 16)
                last = fscr[ch, pl.ds(at, 16), 128 - 128 * (n % 2) : 256 - 128 * (n % 2)]
                fresh = jnp.where(lane16 >= sub16, this, last)
                tiles = [fresh]
                for g in range(1, 8):
                    picked = jnp.where(lane16 < 128 - 16 * g, fresh, last)
                    tiles.append(pltpu.roll(picked, 16 * g, 1))
                u[ch, n + 1] = jnp.concatenate(tiles, axis=0)

    def convolve(q, u, late):
        skipped = 128 if late else 0
        at = pl.multiple_of(256 - 32 * q + skipped, 16)
        low = pl.multiple_of(240 - 32 * q + skipped, 16)
        count = 256 - skipped
        for ch in range(2):
            left = jnp.concatenate(
                [
                    spad[ch, pl.ds(at, count), :],
                    spad_odd[ch, pl.ds(at, count), :],
                    spad[ch, pl.ds(low, count), :],
                    spad_odd[ch, pl.ds(low, count), :],
                ],
                axis=1,
            )
            right = []
            for k in range(4):
                right.append(jnp.concatenate([u[ch, 2 * k + 1], u[ch, 2 * k + 2]], axis=1))
                right.append(jnp.concatenate([u[ch, 2 * k], u[ch, 2 * k + 1]], axis=1))
            acc[ch, skipped:256, :] += mm(left, jnp.concatenate(right, axis=0))

    def correlate(q, c, c_before, late):
        count = 128 if late else 256
        for ch in range(2):
            c[ch, 0] = c_before[ch, 8]
            for s in range(4):
                at = pl.multiple_of(32 * q + 16 * (s // 2), 16)
                right = jnp.concatenate(
                    [gs[4 * ch + (2 * s + odd) % 4, pl.ds(at, count), :] for odd in range(2)],
                    axis=1,
                )
                both = mm(x_revs[ch][:, 0:count], right)
                c[ch, 2 * s + 1] = both[:, 0:128]
                c[ch, 2 * s + 2] = both[:, 128:256]

    def diagonals(c, ch, n):
        part = None
        for g in range(16):
            old = c[ch, n, 8 * g : 8 * g + 8, :]
            new = jnp.zeros((8, 128), F32) if n == 8 else c[ch, n + 1, 8 * g : 8 * g + 8, :]
            now = pltpu.roll(jnp.where(lane + sub >= 127 - 8 * g, old, new), 8 * g + 1, 1)
            part = now if part is None else part + now
        return part

    def sum_diagonals(q, c):
        for ch in range(2):
            for n in range(8):
                to = pl.multiple_of(64 * q + 64 + 8 * n, 8)
                gsc[ch, pl.ds(to, 8), :] = diagonals(c, ch, n)

    build_toeplitz(0, u_a)

    def step(r, late):
        q = 2 * r
        convolve(q, u_a, late)
        correlate(q, c_a, c_b, late)
        build_toeplitz(q + 1, u_b)
        if r > 0:
            sum_diagonals(q - 1, c_b)
        convolve(q + 1, u_b, late)
        correlate(q + 1, c_b, c_a, late)
        if r < 3:
            build_toeplitz(q + 2, u_a)
        sum_diagonals(q, c_a)

    def run_step(late):
        def run(r, carry):
            step(r, late)
            return carry

        return run

    for r in range(4):
        step(r, r >= 2)
    sum_diagonals(7, c_b)

    for ch in range(2):
        mine = iota((1, 256), 1) == own + 128 * ch
        skip_now = jnp.sum(jnp.where(mine, skip[...], 0.0), axis=1, keepdims=True)
        done = (acc[ch] + skip_now * mixed_up[ch]).astype(BF16)
        apart = mm(back, done)
        conv2 = apart[0:128, :]
        gm2 = mm(apart[128:256, :].astype(BF16), rev256)
        for h in range(2):
            osc[pl.ds(2 * ch + h, 128, stride=10), :] = conv2[:, 128 * h : 128 * h + 128]
            osc[pl.ds(4 + 2 * ch + h, 128, stride=10), :] = gm2[:, 128 * h : 128 * h + 128]
        gsc[ch, 576:584, :] = diagonals(c_b, ch, 8)
        gf = row_rolls(gsc[ch, 72:584, :], 3).reshape(64, 8, 128).sum(axis=1)
        osc[pl.ds(8 + ch, 128, stride=10), :] = mm(spread_g, gf.astype(BF16))
    out[...] = osc[0:1280, :].astype(BF16)


def backward_kernel(
    recv, go, gi, v, gg, tok, og, emb, pre1, act1, pre2, act2, bias, modul, hw, fw, sf,
    gp_o, kept, given, scr, tmp, sm, ssc,
):
    own = own_index()
    scr[0:1280, :] = recv[...].astype(F32)

    def line(r):
        return scr[pl.ds(r, 128, stride=10), :]

    def whole(at):
        return jnp.concatenate(
            [
                jnp.concatenate([line(at + 2 * ch), line(at + 2 * ch + 1)], axis=1)
                for ch in range(2)
            ],
            axis=0,
        )

    conv = whole(0).T
    gm = whole(4).T
    gated_t = (go[...].astype(F32) * conv).T.astype(BF16)
    grad_ow = mm(gated_t, og[...])
    gp = jnp.concatenate(
        [
            (gg[...].astype(F32) * conv).astype(BF16),
            (gm * v[...].astype(F32)).astype(BF16),
            (gm * gi[...].astype(F32)).astype(BF16),
        ],
        axis=1,
    )
    gp_o[...] = gp
    grad_iw = mm(tok[...].astype(F32).T.astype(BF16), gp)
    for rb in range(2):
        for cb in range(8):
            src = grad_iw if cb < 6 else grad_ow
            at = 128 * (cb if cb < 6 else cb - 6)
            ssc[pl.ds(8 * rb + cb, 128, stride=18), :] = src[
                128 * rb : 128 * rb + 128, at : at + 128
            ]

    tmp[...] = jnp.concatenate([line(8), line(9)], axis=0).T
    gf = tmp[pl.ds(pl.multiple_of((own % 2) * 64, 64), 64), :]
    gk = gf * modul[...]
    grad_fw = mm_full(act2[...].T, gk)
    ga2 = mm_full(gk, fw[...], NT)
    cos2 = jnp.cos(sf[1:2, :] * pre2[...])
    gp2 = ga2 * sf[1:2, :] * cos2
    grad_f2 = jnp.sum(ga2 * pre2[...] * cos2, axis=0, keepdims=True)
    grad_hb = jnp.sum(gp2, axis=0, keepdims=True)
    grad_hw = mm_full(act1[...].T, gp2)
    ga1 = mm_full(gp2, hw[...], NT)
    cos1 = jnp.cos(sf[0:1, :] * pre1[...])
    gp1 = ga1 * sf[0:1, :] * cos1
    grad_f1 = jnp.sum(ga1 * pre1[...] * cos1, axis=0, keepdims=True)
    grad_eb = jnp.sum(gp1, axis=0, keepdims=True)
    sm[...] = jnp.zeros((128, 128), F32)
    sm[0:64, 0:64] = grad_hw
    for k in range(5):
        sm[64 + k : 65 + k, 0:64] = jnp.sum(emb[k] * gp1, axis=0, keepdims=True)
    sm[69:70, 0:64] = grad_eb
    sm[70:71, 0:64] = grad_hb
    sm[71:72, 0:64] = grad_f1
    sm[72:73, 0:64] = grad_f2
    sm[73:74, :] = bias[:, 0:128]
    sm[74:75, :] = bias[:, 128:256]
    ssc[pl.ds(16, 64, stride=18), :] = grad_fw[:, 0:128]
    ssc[pl.ds(16 + 64 * 18, 64, stride=18), :] = grad_fw[:, 128:256]
    ssc[pl.ds(17, 128, stride=18), :] = sm[...]
    core = own % 2
    kept[...] = ssc[pl.ds(pl.multiple_of(core * 1152, 1152), 1152), :]
    given[...] = ssc[pl.ds(pl.multiple_of((1 - core) * 1152, 1152), 1152), :].astype(BF16)


def token_kernel(gp, wi, gtok):
    gtok[...] = mm(gp[...], wi[...], NT).astype(BF16)


def pair_kernel(kept, taken, out):
    out[...] = (kept[...] + taken[...].astype(F32)).astype(BF16)


def mod18(x):
    return x - 18 * jnp.floor((x.astype(F32) + 0.5) / 18.0).astype(jnp.int32)


def sum_kernel(recv, out):
    pick = one_hot(mod18(iota((32, 1152), 1)) == iota((32, 1152), 0))
    total = mm(pick, recv[...]).astype(BF16)
    again = one_hot(mod18(iota((144, 32), 0)) == iota((144, 32), 1))
    block = mm(again, total).astype(BF16)
    for k in range(8):
        out[144 * k : 144 * k + 144, :] = block


def unpack_kernel(own_core, other, giw, gow, gsb, gew, geb, ghw, ghb, gfw, gsf, scr, small):
    scale = 1.0 / math.sqrt(4 * LENGTH)
    fscale = scale / 4.0
    core = own_index() % 2
    for k, recv in enumerate((own_core, other)):
        scr[k, 0:1152, :] = recv[...].astype(F32)
        first = pl.multiple_of(64 * (core if k == 0 else 1 - core), 64)
        for rb in range(2):
            for cb in range(8):
                tile = scr[k, pl.ds(8 * rb + cb, 64, stride=18), :] * scale
                rows = pl.ds(128 * rb + first, 64)
                if cb < 6:
                    giw[rows, 128 * cb : 128 * cb + 128] = tile
                else:
                    gow[rows, 128 * (cb - 6) : 128 * (cb - 6) + 128] = tile
        for n in range(2):
            small[n, pl.ds(first, 64), :] = scr[k, pl.ds(16 + n, 64, stride=18), :]
    gfw[:, 0:128] = small[0, 0:64, :] * fscale
    gfw[:, 128:256] = small[0, 64:128, :] * fscale
    second = small[1]
    ghw[...] = second[0:64, 0:64] * fscale
    gew[...] = second[64:69, 0:64] * fscale
    geb[...] = second[69:70, 0:64] * fscale
    ghb[...] = second[70:71, 0:64] * fscale
    gsf[...] = second[71:73, 0:64] * fscale
    gsb[:, 0:128] = second[73:74, :] * scale
    gsb[:, 128:256] = second[74:75, :] * scale


def call(kernel, name, out_shape, scratch=(), from_hbm=False):
    def run(*args):
        return pl.pallas_call(
            kernel,
            out_shape=out_shape,
            in_specs=[
                pl.BlockSpec(memory_space=pltpu.HBM if from_hbm else pltpu.VMEM) for _ in args
            ],
            scratch_shapes=list(scratch),
            compiler_params=pltpu.CompilerParams(vmem_limit_bytes=48 * 1024 * 1024),
            name=name,
        )(*args)

    return run


def conv_scratch():
    return [
        pltpu.VMEM((1296, 128), F32),
        pltpu.VMEM((1296, 128), F32),
        pltpu.VMEM((2, 592, 256), BF16),
        pltpu.VMEM((2, 9, 128, 128), BF16),
        pltpu.VMEM((2, 9, 128, 128), BF16),
        pltpu.VMEM((2, 9, 128, 128), F32),
        pltpu.VMEM((2, 9, 128, 128), F32),
        pltpu.VMEM((2, 512, 256), BF16),
        pltpu.VMEM((2, 512, 256), BF16),
        pltpu.VMEM((2, 256, 256), F32),
        pltpu.VMEM((2, 272, 128), F32),
        pltpu.VMEM((8, 384, 128), BF16),
        pltpu.VMEM((2, 584, 128), F32),
    ]


def exchange(x, rows, groups=None):
    count = x.shape[0] // rows
    y = x.reshape(count, rows // 2, 2, 128)
    y = lax.all_to_all(
        y, AXES, split_axis=0, concat_axis=0, axis_index_groups=groups, tiled=True
    )
    return y.reshape(count * rows, 128)


def swap_cores(x):
    return lax.ppermute(x, "batch", [(k, k ^ 1) for k in range(4)])


def sds(*shape, dtype=F32):
    return jax.ShapeDtypeStruct(shape, dtype)


def shards(
    tokens, out_grad, in_weight, out_weight, skip_bias, embed_weight, embed_bias,
    hidden_weight, hidden_bias, filter_weight, sine_freq, decay_rate,
):
    tok = tokens[0]
    og = out_grad[0]
    decay = decay_rate[None, :]
    square = sds(256, 256, dtype=BF16)
    hidden = sds(64, 64)
    inputs = (tok, og, in_weight, out_weight, embed_weight, embed_bias[None, :], hidden_weight,
              hidden_bias[None, :], filter_weight, sine_freq, decay, skip_bias[None, :])
    (slab, go, gi, v, gg, bias, emb, pre1, act1, pre2, act2,
     skip, modul, hw, fw, sf) = call(
        forward_kernel,
        "forward",
        (sds(1280, 128, dtype=BF16), square, square, square, square, sds(1, 256),
         sds(5, 64, 64), hidden, hidden, hidden, hidden, sds(1, 256),
         sds(64, 256), hidden, sds(64, 256), sds(2, 64)),
        [pltpu.VMEM(x.shape, x.dtype) for x in inputs]
        + [pltpu.VMEM((1296, 128), F32), pltpu.SemaphoreType.DMA((len(inputs),))],
        from_hbm=True,
    )(*(pltpu.with_memory_space_constraint(x, pltpu.HBM) for x in inputs))
    recv = exchange(slab, 10)
    sent = call(
        conv_kernel,
        "conv",
        sds(1280, 128, dtype=BF16),
        conv_scratch(),
    )(recv, skip)
    recv = exchange(sent, 10)
    gp, kept, given = call(
        backward_kernel,
        "backward",
        (sds(256, 768, dtype=BF16), sds(1152, 128), sds(1152, 128, dtype=BF16)),
        [
            pltpu.VMEM((1296, 128), F32),
            pltpu.VMEM((128, 256), F32),
            pltpu.VMEM((128, 128), F32),
            pltpu.VMEM((2336, 128), F32),
        ],
    )(recv, go, gi, v, gg, tok, og, emb, pre1, act1, pre2, act2, bias, modul, hw, fw, sf)
    gtok = call(token_kernel, "tokens", square)(gp, in_weight)
    half = sds(1152, 128, dtype=BF16)
    slab = call(pair_kernel, "pair", half)(kept, swap_cores(given))
    by_core = [list(range(core, 128, 2)) for core in range(2)]
    recv = exchange(slab, 18, by_core)
    total = call(sum_kernel, "total", half)(recv)
    recv = exchange(total, 18, by_core)
    giw, gow, gsb, gew, geb, ghw, ghb, gfw, gsf = call(
        unpack_kernel,
        "unpack",
        (sds(256, 768), sds(256, 256), sds(1, 256), sds(5, 64), sds(1, 64), sds(64, 64),
         sds(1, 64), sds(64, 256), sds(2, 64)),
        [pltpu.VMEM((2, 1184, 128), F32), pltpu.VMEM((2, 128, 128), F32)],
    )(recv, swap_cores(recv))
    return (gtok[None], giw, gow, gsb[0], gew, geb[0], ghw, ghb[0], gfw, gsf)


def solution(mesh):
    return jax.shard_map(
        shards,
        mesh=mesh,
        in_specs=(P("batch", "seq", None),) * 2 + (P(),) * 10,
        out_specs=(P("batch", "seq", None),) + (P(),) * 9,
        check_vma=False,
    )
```

```python
import math

import jax
import jax.numpy as jnp
from jax import lax
from jax.experimental import pallas as pl
from jax.experimental.pallas import tpu as pltpu
from jax.sharding import PartitionSpec as P

F32 = jnp.float32
BF16 = jnp.bfloat16
HIGHEST = lax.Precision.HIGHEST
AXES = ("seq", "batch")
LENGTH = 8192
BANDS = 2
NN = (((1,), (0,)), ((), ()))
NT = (((1,), (1,)), ((), ()))


def mm(a, b, dims=NN):
    return lax.dot_general(a, b, dims, preferred_element_type=F32)


def mm_full(a, b, dims=NN):
    return lax.dot_general(a, b, dims, precision=HIGHEST, preferred_element_type=F32)


def iota(shape, dim):
    return lax.broadcasted_iota(jnp.int32, shape, dim)


def one_hot(cond):
    return jnp.where(cond, 1.0, 0.0).astype(BF16)


def own_index():
    return lax.axis_index("seq") * lax.axis_size("batch") + lax.axis_index("batch")


def modulation(decay, first, shape):
    pos = (first + iota(shape, 0)).astype(F32)
    return 4.0 * jnp.exp(-decay * pos) / math.sqrt(LENGTH)


def forward_kernel(
    tok_h, og_h, wi_h, wo_h, ew_h, eb_h, hw_h, hb_h, fw_h, sf_h, dr_h, sk_h,
    slab, go_o, gi_o, v_o, gg_o, bias_o, emb_o, pre1_o, act1_o, pre2_o, act2_o,
    sk_o, mod_o, hw_o, fw_o, sf_o,
    tok, og, wi, wo, ew, eb, hw, hb, fw, sf, dr, sk, scr, sems,
):
    pairs = (
        (ew_h, ew), (eb_h, eb), (sf_h, sf), (hw_h, hw), (hb_h, hb), (wi_h, wi), (tok_h, tok),
        (og_h, og), (wo_h, wo), (fw_h, fw), (dr_h, dr), (sk_h, sk),
    )
    copies = [pltpu.make_async_copy(a, b, sems.at[k]) for k, (a, b) in enumerate(pairs)]
    for c in copies:
        c.start()
    first = own_index() * 64
    scaled = (first + iota((64, 64), 0)).astype(F32) / LENGTH
    rows = [scaled]
    for band in range(1, BANDS + 1):
        angle = 2.0 * math.pi * band * scaled
        rows.append(jnp.cos(angle))
        rows.append(jnp.sin(angle))
    for c in copies[0:5]:
        c.wait()
    pre1 = eb[...]
    for k in range(5):
        pre1 = pre1 + rows[k] * ew[k : k + 1, :]
        emb_o[k] = rows[k]
    act1 = jnp.sin(sf[0:1, :] * pre1)
    pre2 = mm_full(act1, hw[...]) + hb[...]
    for c in copies[5:]:
        c.wait()
    proj = mm(tok[...], wi[...])
    go = proj[:, :256].astype(BF16)
    gi = proj[:, 256:512].astype(BF16)
    v = proj[:, 512:].astype(BF16)
    gg = mm(og[...], wo[...], NT).astype(BF16)
    go_o[...] = go
    gi_o[...] = gi
    v_o[...] = v
    gg_o[...] = gg
    mixed = (v.astype(F32) * gi.astype(F32)).astype(BF16).astype(F32)
    gc = (gg.astype(F32) * go.astype(F32)).astype(BF16).astype(F32)
    sk_o[...] = sk[...]
    hw_o[...] = hw[...]
    fw_o[...] = fw[...]
    sf_o[...] = sf[...]
    bias_o[...] = jnp.sum(gc * mixed, axis=0, keepdims=True)
    mixed_t = mixed.T
    gc_t = gc.T
    act2 = jnp.sin(sf[1:2, :] * pre2)
    pre1_o[...] = pre1
    act1_o[...] = act1
    pre2_o[...] = pre2
    act2_o[...] = act2
    modul = modulation(dr[...], first, (64, 256))
    mod_o[...] = modul
    filt = mm_full(act2, fw[...]) * modul
    side = 64 * (lax.axis_index("batch") % 2)
    place = one_hot(iota((64, 128), 1) == iota((64, 128), 0) + side)
    filt_t = mm(filt.T.astype(BF16), place)
    for ch in range(2):
        scr[pl.ds(8 + ch, 128, stride=10), :] = filt_t[128 * ch : 128 * ch + 128, :]
        for at, whole in ((0, mixed_t), (4, gc_t)):
            for half in range(2):
                scr[pl.ds(at + 2 * ch + half, 128, stride=10), :] = whole[
                    128 * ch : 128 * ch + 128, 128 * half : 128 * half + 128
                ]
    slab[...] = scr[0:1280, :].astype(BF16)


def row_rolls(x, bits):
    row = iota(x.shape, 0)
    for bit in range(bits):
        x = jnp.where((row >> bit) & 1 == 1, pltpu.roll(x, 1 << bit, 1), x)
    return x


def conv_kernel(
    recv, skip, out, scr, osc, fscr, u_a, u_b, c_a, c_b, spad, spad_odd, acc, gpad, gs, gsc
):
    scr[0:1280, :] = recv[...].astype(F32)
    own = own_index()
    row, col = iota((256, 256), 0), iota((256, 256), 1)
    rev256 = one_hot(row + col == 255)
    rev128 = one_hot(iota((128, 128), 0) + iota((128, 128), 1) == 127)

    def source(r):
        blk, sig = r >> 3, r & 7
        return jnp.where(sig < 4, blk * 4 + sig, 128 + (31 - blk) * 4 + sig - 4)

    perm = one_hot(source(row) == col)
    weave = one_hot(((row >> 2) & 1) * 128 + (row >> 3) * 4 + (row & 3) == col)
    back = one_hot(source(col) == row)
    gather = [
        one_hot(iota((512, 128), 1) >> 1 == 2 * (iota((512, 128), 0) >> 4) + h) for h in range(2)
    ]
    spread_g = one_hot(iota((128, 64), 0) >> 1 == iota((128, 64), 1))
    lane, sub = iota((8, 128), 1), iota((8, 128), 0)
    lane16, sub16 = iota((16, 128), 1), iota((16, 128), 0)

    def line(r):
        return scr[pl.ds(r, 128, stride=10), :]

    mixed_up, x_revs = [], []
    for ch in range(2):
        f_in = line(8 + ch).astype(BF16)
        fscr[ch, 0:16, :] = jnp.zeros((16, 256), BF16)
        fscr[ch, 528:592, :] = jnp.zeros((64, 256), BF16)
        for h in range(2):
            fscr[ch, 16:528, 128 * h : 128 * h + 128] = row_rolls(mm(gather[h], f_in), 4).astype(BF16)
    for ch in range(2):
        xs = [line(2 * ch + h) for h in range(2)]
        gs_in = [line(4 + 2 * ch + h) for h in range(2)]
        x2 = jnp.concatenate(xs, axis=1).astype(BF16)
        g2 = jnp.concatenate(gs_in, axis=1).astype(BF16)
        g_rev = mm(g2, rev256).astype(BF16)
        up = mm(perm, jnp.concatenate([x2, g_rev], axis=0))
        mixed_up.append(up)
        spad[ch, 0:256, :] = jnp.zeros((256, 256), BF16)
        spad_odd[ch, 0:256, :] = jnp.zeros((256, 256), BF16)
        spad[ch, 256:512, :] = up.astype(BF16)
        spad_odd[ch, 256:512, :] = jnp.concatenate(
            [jnp.zeros((8, 256), F32), up[0:248, :]], axis=0
        ).astype(BF16)
        acc[ch] = jnp.zeros((256, 256), F32)
        c_b[ch, 8] = jnp.zeros((128, 128), F32)
        woven = mm(
            weave,
            jnp.concatenate(
                [jnp.concatenate([xs[h], gs_in[h]], axis=1) for h in range(2)], axis=0
            ).astype(BF16),
        )
        x_revs.append(mm(rev128, woven[:, 0:128].astype(BF16), NT).astype(BF16))
        gpad[ch, 0:256, :] = woven[:, 128:256]
        gpad[ch, 256:272, :] = jnp.zeros((16, 128), F32)
        for s in range(4):
            gs[4 * ch + s, 0:256, :] = gpad[ch, 4 * s : 4 * s + 256, :].astype(BF16)
            gs[4 * ch + s, 256:384, :] = jnp.zeros((128, 128), BF16)

    def build_toeplitz(q, u):
        for ch in range(2):
            for n in range(-1, 8):
                at = pl.multiple_of(64 * q + 16 * (n // 2 + 1), 16)
                this = fscr[ch, pl.ds(at, 16), 128 * (n % 2) : 128 * (n % 2) + 128]
                at = pl.multiple_of(64 * q + 16 * ((n - 1) // 2 + 1), 16)
                last = fscr[ch, pl.ds(at, 16), 128 - 128 * (n % 2) : 256 - 128 * (n % 2)]
                fresh = jnp.where(lane16 >= sub16, this, last)
                tiles = [fresh]
                for g in range(1, 8):
                    picked = jnp.where(lane16 < 128 - 16 * g, fresh, last)
                    tiles.append(pltpu.roll(picked, 16 * g, 1))
                u[ch, n + 1] = jnp.concatenate(tiles, axis=0)

    def convolve(q, u, late):
        skipped = 128 if late else 0
        at = pl.multiple_of(256 - 32 * q + skipped, 16)
        low = pl.multiple_of(240 - 32 * q + skipped, 16)
        count = 256 - skipped
        for ch in range(2):
            left = jnp.concatenate(
                [
                    spad[ch, pl.ds(at, count), :],
                    spad_odd[ch, pl.ds(at, count), :],
                    spad[ch, pl.ds(low, count), :],
                    spad_odd[ch, pl.ds(low, count), :],
                ],
                axis=1,
            )
            right = []
            for k in range(4):
                right.append(jnp.concatenate([u[ch, 2 * k + 1], u[ch, 2 * k + 2]], axis=1))
                right.append(jnp.concatenate([u[ch, 2 * k], u[ch, 2 * k + 1]], axis=1))
            acc[ch, skipped:256, :] += mm(left, jnp.concatenate(right, axis=0))

    def correlate(q, c, c_before, late):
        count = 128 if late else 256
        for ch in range(2):
            c[ch, 0] = c_before[ch, 8]
            for s in range(4):
                at = pl.multiple_of(32 * q + 16 * (s // 2), 16)
                right = jnp.concatenate(
                    [gs[4 * ch + (2 * s + odd) % 4, pl.ds(at, count), :] for odd in range(2)],
                    axis=1,
                )
                both = mm(x_revs[ch][:, 0:count], right)
                c[ch, 2 * s + 1] = both[:, 0:128]
                c[ch, 2 * s + 2] = both[:, 128:256]

    def diagonals(c, ch, n):
        part = None
        for g in range(16):
            old = c[ch, n, 8 * g : 8 * g + 8, :]
            new = jnp.zeros((8, 128), F32) if n == 8 else c[ch, n + 1, 8 * g : 8 * g + 8, :]
            now = pltpu.roll(jnp.where(lane + sub >= 127 - 8 * g, old, new), 8 * g + 1, 1)
            part = now if part is None else part + now
        return part

    def sum_diagonals(q, c):
        for ch in range(2):
            for n in range(8):
                to = pl.multiple_of(64 * q + 64 + 8 * n, 8)
                gsc[ch, pl.ds(to, 8), :] = diagonals(c, ch, n)

    build_toeplitz(0, u_a)

    def step(r, late):
        q = 2 * r
        convolve(q, u_a, late)
        correlate(q, c_a, c_b, late)
        build_toeplitz(q + 1, u_b)
        if r > 0:
            sum_diagonals(q - 1, c_b)
        convolve(q + 1, u_b, late)
        correlate(q + 1, c_b, c_a, late)
        if r < 3:
            build_toeplitz(q + 2, u_a)
        sum_diagonals(q, c_a)

    def run_step(late):
        def run(r, carry):
            step(r, late)
            return carry

        return run

    for r in range(4):
        step(r, r >= 2)
    sum_diagonals(7, c_b)

    for ch in range(2):
        mine = iota((1, 256), 1) == own + 128 * ch
        skip_now = jnp.sum(jnp.where(mine, skip[...], 0.0), axis=1, keepdims=True)
        done = (acc[ch] + skip_now * mixed_up[ch]).astype(BF16)
        apart = mm(back, done)
        conv2 = apart[0:128, :]
        gm2 = mm(apart[128:256, :].astype(BF16), rev256)
        for h in range(2):
            osc[pl.ds(2 * ch + h, 128, stride=10), :] = conv2[:, 128 * h : 128 * h + 128]
            osc[pl.ds(4 + 2 * ch + h, 128, stride=10), :] = gm2[:, 128 * h : 128 * h + 128]
        gsc[ch, 576:584, :] = diagonals(c_b, ch, 8)
        gf = row_rolls(gsc[ch, 72:584, :], 3).reshape(64, 8, 128).sum(axis=1)
        osc[pl.ds(8 + ch, 128, stride=10), :] = mm(spread_g, gf.astype(BF16))
    out[...] = osc[0:1280, :].astype(BF16)


def backward_kernel(
    recv, go, gi, v, gg, tok, og, emb, pre1, act1, pre2, act2, bias, modul, hw, fw, sf,
    gp_o, kept, given, scr, tmp, sm, ssc,
):
    own = own_index()
    scr[0:1280, :] = recv[...].astype(F32)

    def line(r):
        return scr[pl.ds(r, 128, stride=10), :]

    def whole(at):
        return jnp.concatenate(
            [
                jnp.concatenate([line(at + 2 * ch), line(at + 2 * ch + 1)], axis=1)
                for ch in range(2)
            ],
            axis=0,
        )

    conv = whole(0).T
    gm = whole(4).T
    gated_t = (go[...].astype(F32) * conv).T.astype(BF16)
    grad_ow = mm(gated_t, og[...])
    gp = jnp.concatenate(
        [
            (gg[...].astype(F32) * conv).astype(BF16),
            (gm * v[...].astype(F32)).astype(BF16),
            (gm * gi[...].astype(F32)).astype(BF16),
        ],
        axis=1,
    )
    gp_o[...] = gp
    grad_iw = mm(tok[...].astype(F32).T.astype(BF16), gp)
    for rb in range(2):
        for cb in range(8):
            src = grad_iw if cb < 6 else grad_ow
            at = 128 * (cb if cb < 6 else cb - 6)
            ssc[pl.ds(8 * rb + cb, 128, stride=18), :] = src[
                128 * rb : 128 * rb + 128, at : at + 128
            ]

    tmp[...] = jnp.concatenate([line(8), line(9)], axis=0).T
    gf = tmp[pl.ds(pl.multiple_of((own % 2) * 64, 64), 64), :]
    gk = gf * modul[...]
    grad_fw = mm_full(act2[...].T, gk)
    ga2 = mm_full(gk, fw[...], NT)
    cos2 = jnp.cos(sf[1:2, :] * pre2[...])
    gp2 = ga2 * sf[1:2, :] * cos2
    grad_f2 = jnp.sum(ga2 * pre2[...] * cos2, axis=0, keepdims=True)
    grad_hb = jnp.sum(gp2, axis=0, keepdims=True)
    grad_hw = mm_full(act1[...].T, gp2)
    ga1 = mm_full(gp2, hw[...], NT)
    cos1 = jnp.cos(sf[0:1, :] * pre1[...])
    gp1 = ga1 * sf[0:1, :] * cos1
    grad_f1 = jnp.sum(ga1 * pre1[...] * cos1, axis=0, keepdims=True)
    grad_eb = jnp.sum(gp1, axis=0, keepdims=True)
    sm[...] = jnp.zeros((128, 128), F32)
    sm[0:64, 0:64] = grad_hw
    for k in range(5):
        sm[64 + k : 65 + k, 0:64] = jnp.sum(emb[k] * gp1, axis=0, keepdims=True)
    sm[69:70, 0:64] = grad_eb
    sm[70:71, 0:64] = grad_hb
    sm[71:72, 0:64] = grad_f1
    sm[72:73, 0:64] = grad_f2
    sm[73:74, :] = bias[:, 0:128]
    sm[74:75, :] = bias[:, 128:256]
    ssc[pl.ds(16, 64, stride=18), :] = grad_fw[:, 0:128]
    ssc[pl.ds(16 + 64 * 18, 64, stride=18), :] = grad_fw[:, 128:256]
    ssc[pl.ds(17, 128, stride=18), :] = sm[...]
    core = own % 2
    kept[...] = ssc[pl.ds(pl.multiple_of(core * 1152, 1152), 1152), :]
    given[...] = ssc[pl.ds(pl.multiple_of((1 - core) * 1152, 1152), 1152), :].astype(BF16)


def token_kernel(gp, wi, gtok):
    gtok[...] = mm(gp[...], wi[...], NT).astype(BF16)


def pair_kernel(kept, taken, out):
    out[...] = (kept[...] + taken[...].astype(F32)).astype(BF16)


def mod18(x):
    return x - 18 * jnp.floor((x.astype(F32) + 0.5) / 18.0).astype(jnp.int32)


def sum_kernel(recv, out):
    pick = one_hot(mod18(iota((32, 1152), 1)) == iota((32, 1152), 0))
    total = mm(pick, recv[...]).astype(BF16)
    again = one_hot(mod18(iota((144, 32), 0)) == iota((144, 32), 1))
    block = mm(again, total).astype(BF16)
    for k in range(8):
        out[144 * k : 144 * k + 144, :] = block


def unpack_kernel(own_core, other, giw, gow, gsb, gew, geb, ghw, ghb, gfw, gsf, scr, small):
    scale = 1.0 / math.sqrt(4 * LENGTH)
    fscale = scale / 4.0
    core = own_index() % 2
    for k, recv in enumerate((own_core, other)):
        scr[k, 0:1152, :] = recv[...].astype(F32)
        first = pl.multiple_of(64 * (core if k == 0 else 1 - core), 64)
        for rb in range(2):
            for cb in range(8):
                tile = scr[k, pl.ds(8 * rb + cb, 64, stride=18), :] * scale
                rows = pl.ds(128 * rb + first, 64)
                if cb < 6:
                    giw[rows, 128 * cb : 128 * cb + 128] = tile
                else:
                    gow[rows, 128 * (cb - 6) : 128 * (cb - 6) + 128] = tile
        for n in range(2):
            small[n, pl.ds(first, 64), :] = scr[k, pl.ds(16 + n, 64, stride=18), :]
    gfw[:, 0:128] = small[0, 0:64, :] * fscale
    gfw[:, 128:256] = small[0, 64:128, :] * fscale
    second = small[1]
    ghw[...] = second[0:64, 0:64] * fscale
    gew[...] = second[64:69, 0:64] * fscale
    geb[...] = second[69:70, 0:64] * fscale
    ghb[...] = second[70:71, 0:64] * fscale
    gsf[...] = second[71:73, 0:64] * fscale
    gsb[:, 0:128] = second[73:74, :] * scale
    gsb[:, 128:256] = second[74:75, :] * scale


def call(kernel, name, out_shape, scratch=(), from_hbm=False):
    def run(*args):
        return pl.pallas_call(
            kernel,
            out_shape=out_shape,
            in_specs=[
                pl.BlockSpec(memory_space=pltpu.HBM if from_hbm else pltpu.VMEM) for _ in args
            ],
            scratch_shapes=list(scratch),
            compiler_params=pltpu.CompilerParams(vmem_limit_bytes=48 * 1024 * 1024),
            name=name,
        )(*args)

    return run


def conv_scratch():
    return [
        pltpu.VMEM((1296, 128), F32),
        pltpu.VMEM((1296, 128), F32),
        pltpu.VMEM((2, 592, 256), BF16),
        pltpu.VMEM((2, 9, 128, 128), BF16),
        pltpu.VMEM((2, 9, 128, 128), BF16),
        pltpu.VMEM((2, 9, 128, 128), F32),
        pltpu.VMEM((2, 9, 128, 128), F32),
        pltpu.VMEM((2, 512, 256), BF16),
        pltpu.VMEM((2, 512, 256), BF16),
        pltpu.VMEM((2, 256, 256), F32),
        pltpu.VMEM((2, 272, 128), F32),
        pltpu.VMEM((8, 384, 128), BF16),
        pltpu.VMEM((2, 584, 128), F32),
    ]


def exchange(x, rows, groups=None):
    count = x.shape[0] // rows
    y = x.reshape(count, rows // 2, 2, 128)
    y = lax.all_to_all(
        y, AXES, split_axis=0, concat_axis=0, axis_index_groups=groups, tiled=True
    )
    return y.reshape(count * rows, 128)


def swap_cores(x):
    return lax.ppermute(x, "batch", [(k, k ^ 1) for k in range(4)])


def sds(*shape, dtype=F32):
    return jax.ShapeDtypeStruct(shape, dtype)


def shards(
    tokens, out_grad, in_weight, out_weight, skip_bias, embed_weight, embed_bias,
    hidden_weight, hidden_bias, filter_weight, sine_freq, decay_rate,
):
    tok = tokens[0]
    og = out_grad[0]
    decay = decay_rate[None, :]
    square = sds(256, 256, dtype=BF16)
    hidden = sds(64, 64)
    inputs = (tok, og, in_weight, out_weight, embed_weight, embed_bias[None, :], hidden_weight,
              hidden_bias[None, :], filter_weight, sine_freq, decay, skip_bias[None, :])
    (slab, go, gi, v, gg, bias, emb, pre1, act1, pre2, act2,
     skip, modul, hw, fw, sf) = call(
        forward_kernel,
        "forward",
        (sds(1280, 128, dtype=BF16), square, square, square, square, sds(1, 256),
         sds(5, 64, 64), hidden, hidden, hidden, hidden, sds(1, 256),
         sds(64, 256), hidden, sds(64, 256), sds(2, 64)),
        [pltpu.VMEM(x.shape, x.dtype) for x in inputs]
        + [pltpu.VMEM((1296, 128), F32), pltpu.SemaphoreType.DMA((len(inputs),))],
        from_hbm=True,
    )(*(pltpu.with_memory_space_constraint(x, pltpu.HBM) for x in inputs))
    recv = exchange(slab, 10)
    sent = call(
        conv_kernel,
        "conv",
        sds(1280, 128, dtype=BF16),
        conv_scratch(),
    )(recv, skip)
    recv = exchange(sent, 10)
    gp, kept, given = call(
        backward_kernel,
        "backward",
        (sds(256, 768, dtype=BF16), sds(1152, 128), sds(1152, 128, dtype=BF16)),
        [
            pltpu.VMEM((1296, 128), F32),
            pltpu.VMEM((128, 256), F32),
            pltpu.VMEM((128, 128), F32),
            pltpu.VMEM((2336, 128), F32),
        ],
    )(recv, go, gi, v, gg, tok, og, emb, pre1, act1, pre2, act2, bias, modul, hw, fw, sf)
    gtok = call(token_kernel, "tokens", square)(gp, in_weight)
    half = sds(1152, 128, dtype=BF16)
    slab = call(pair_kernel, "pair", half)(kept, swap_cores(given))
    by_core = [list(range(core, 128, 2)) for core in range(2)]
    recv = exchange(slab, 18, by_core)
    total = call(sum_kernel, "total", half)(recv)
    recv = exchange(total, 18, by_core)
    giw, gow, gsb, gew, geb, ghw, ghb, gfw, gsf = call(
        unpack_kernel,
        "unpack",
        (sds(256, 768), sds(256, 256), sds(1, 256), sds(5, 64), sds(1, 64), sds(64, 64),
         sds(1, 64), sds(64, 256), sds(2, 64)),
        [pltpu.VMEM((2, 1184, 128), F32), pltpu.VMEM((2, 128, 128), F32)],
    )(recv, swap_cores(recv))
    return (gtok[None], giw, gow, gsb[0], gew, geb[0], ghw, ghb[0], gfw, gsf)


def solution(mesh):
    return jax.shard_map(
        shards,
        mesh=mesh,
        in_specs=(P("batch", "seq", None),) * 2 + (P(),) * 10,
        out_specs=(P("batch", "seq", None),) + (P(),) * 9,
        check_vma=False,
    )
```
